32 devices in a mesh: dp: 2 (over core), ctx: 4 (over z), head: 4 (over y, x).
Axes of the slice: x: 2, y: 2, z: 4, core: 2. Of those that a mesh axis runs over, the one named last changes fastest.
Arguments:
- tokens: bfloat16 [6144, 1536], P(('dp', 'ctx'), 'head'), may hold values from -6 to 6
- segment_ids: int32 [6144], P('dp'), may hold values from 0 to 1, as said below
- gain_attn: float32 [1536], replicated, may hold values from 0.5 to 1.5
- w_query: bfloat16 [1536, 1536], P(('dp', 'ctx'), 'head'), may hold values from -0.15625 to 0.15625
- w_key: bfloat16 [1536, 1536], P(('dp', 'ctx'), 'head'), may hold values from -0.15625 to 0.15625
- w_value: bfloat16 [1536, 1536], P(('dp', 'ctx'), 'head'), may hold values from -0.15625 to 0.15625
- w_output: bfloat16 [1536, 1536], P('head', ('dp', 'ctx')), may hold values from -0.4375 to 0.4375
- lambda_vec: float32 [4, 64], replicated, may hold values from -1.25 to 1.25
- gain_heads: float32 [128], replicated, may hold values from 0.5 to 1.5
- gain_ffn: float32 [1536], replicated, may hold values from 0.5 to 1.5
- w_gate: bfloat16 [1536, 4096], P(('dp', 'ctx'), 'head'), may hold values from -0.15625 to 0.15625
- w_up: bfloat16 [1536, 4096], P(('dp', 'ctx'), 'head'), may hold values from -0.15625 to 0.15625
- w_down: bfloat16 [4096, 1536], P('head', ('dp', 'ctx')), may hold values from -0.1875 to 0.1875
- grad_out: bfloat16 [6144, 1536], P(('dp', 'ctx'), 'head'), may hold values from -6 to 6
Outputs:
- output: bfloat16 [6144, 1536], P(('dp', 'ctx'), 'head')
- grad_tokens: float32 [6144, 1536], P(('dp', 'ctx'), 'head')
- grad_gain_attn: float32 [1536], replicated
- grad_w_query: float32 [1536, 1536], P(('dp', 'ctx'), 'head')
- grad_w_key: float32 [1536, 1536], P(('dp', 'ctx'), 'head')
- grad_w_value: float32 [1536, 1536], P(('dp', 'ctx'), 'head')
- grad_w_output: float32 [1536, 1536], P('head', ('dp', 'ctx'))
- grad_lambda: float32 [4, 64], replicated
- grad_gain_heads: float32 [128], replicated
- grad_gain_ffn: float32 [1536], replicated
- grad_w_gate: float32 [1536, 4096], P(('dp', 'ctx'), 'head')
- grad_w_up: float32 [1536, 4096], P(('dp', 'ctx'), 'head')
- grad_w_down: float32 [4096, 1536], P('head', ('dp', 'ctx'))
The draws below stay inside these ranges and needn't reach their ends.
Inputs may be any that keep to these rules, and one draw needn't show every extreme that they name: `segment_ids`: within each group of 3072 rows the ids start at 0, never fall, and take every value up to 1; every sequence holds at least 1024 tokens.
All inputs are finite; a program needn't handle non-finite values.
Results may differ from the reference program's by a relative error of at most 0.03.
Values may be sent and summed in bfloat16 or wider, within the bound.
No kernel may reach another device: no remote copies, remote signals or barrier semaphores. Data moves between devices by JAX's collectives and lax.ppermute only.
A program may use at most 192 MiB of HBM per device.

```python
import functools
import math
import jax
import jax.numpy as jnp
from jax import lax

D = 1536
H = 12
HALF = 64
VD = 128
FF = 4096
LAYER = 6
TOK_DEV = 768
GROUP = 3072
SEQS = 2
SEQ_MIN = 1024
TOKENS = 6144
N_CTX = 4


def split_group(group_key):
    spare_rows = GROUP - SEQS * SEQ_MIN
    cut_points = jnp.sort(jax.random.randint(group_key, (SEQS - 1,), 0, spare_rows + 1, dtype=jnp.int32))
    cut_edges = jnp.concatenate([jnp.zeros((1,), jnp.int32), cut_points.astype(jnp.int32), jnp.full((1,), spare_rows, jnp.int32)])
    seq_lengths = SEQ_MIN + cut_edges[1:] - cut_edges[:-1]
    seq_ends = jnp.cumsum(seq_lengths).astype(jnp.int32)
    where_at = jnp.arange(GROUP, dtype=jnp.int32)
    return jnp.sum((where_at[:, None] >= seq_ends[None, :SEQS - 1]).astype(jnp.int32), axis=1)


def draw_segment_ids(key, part):
    group_keys = jax.random.split(key, TOKENS // GROUP)
    return jax.vmap(split_group)(group_keys).reshape(TOKENS).astype(jnp.int32)


def shard_levels(stream_key, extent, pieces, low, largest):
    def one(dim, parts):
        draws = jax.random.uniform(jax.random.fold_in(jax.random.fold_in(stream_key, 6), dim), (parts,), jnp.float32, low / len(pieces), largest / len(pieces))
        return jnp.repeat(jnp.exp(draws), extent[dim] // parts).reshape((-1,) + (1,) * (len(extent) - dim - 1))

    level = one(*pieces[0])
    for cut in pieces[1:]:
        level = level * one(*cut)
    return level


def scatter_about(rng, shape, width, limit, cuts=(), kind=jnp.bfloat16):
    values = width * jax.random.normal(rng, shape, jnp.float32)
    if cuts:
        values = values * shard_levels(rng, shape, cuts, -0.22, 0.18)
    return jnp.clip(values, -limit, limit).astype(kind)


def setup_inputs(seed: int = 0) -> dict:
    splits = jax.random.split(jax.random.key(seed), 15)
    tokens = scatter_about(splits[0], (TOKENS, D), 1.0, 6.0, ((0, 8), (1, 4)))
    segment_ids = draw_segment_ids(jax.random.fold_in(splits[14], 71), 0)
    gain_attn = jnp.clip(1.0 + 0.1 * jax.random.normal(splits[2], (D,), jnp.float32), 0.5, 1.5)
    w_query = scatter_about(splits[3], (D, 2 * H * HALF), D ** -0.5, 0.15625, ((0, 8), (1, 4)))
    w_key = scatter_about(splits[4], (D, 2 * H * HALF), D ** -0.5, 0.15625, ((0, 8), (1, 4)))
    w_value = scatter_about(splits[5], (D, H * VD), D ** -0.5, 0.15625, ((0, 8), (1, 4)))
    w_output = scatter_about(splits[6], (H * VD, D), (H * VD // 9) ** -0.5, 0.4375, ((0, 4), (1, 8)))
    lambda_vec = scatter_about(splits[7], (4, HALF), 0.2, 1.25, (), jnp.float32)
    gain_heads = jnp.clip(1.0 + 0.1 * jax.random.normal(splits[8], (VD,), jnp.float32), 0.5, 1.5)
    gain_ffn = jnp.clip(1.0 + 0.1 * jax.random.normal(splits[9], (D,), jnp.float32), 0.5, 1.5)
    w_gate = scatter_about(splits[10], (D, FF), D ** -0.5, 0.15625, ((0, 8), (1, 4)))
    w_up = scatter_about(splits[11], (D, FF), D ** -0.5, 0.15625, ((0, 8), (1, 4)))
    w_down = scatter_about(splits[12], (FF, D), (FF // 4) ** -0.5, 0.1875, ((0, 4), (1, 8)))
    grad_out = scatter_about(splits[13], (TOKENS, D), 1.0, 6.0, ((0, 8), (1, 4)))
    return {"tokens": tokens, "segment_ids": segment_ids, "gain_attn": gain_attn, "w_query": w_query, "w_key": w_key, "w_value": w_value, "w_output": w_output, "lambda_vec": lambda_vec, "gain_heads": gain_heads, "gain_ffn": gain_ffn, "w_gate": w_gate, "w_up": w_up, "w_down": w_down, "grad_out": grad_out}


EPSILON = 1e-06
ROPE_BASE = 10000.0
NEGATIVE = -1e+30
PRECISE = lax.Precision.HIGHEST

@jax.custom_vjp
def low(v):
    return lax.optimization_barrier(v.astype(jnp.bfloat16)).astype(jnp.float32)

@jax.custom_vjp
def low_back(v):
    return v

def low_keep(v):
    return (low(v), None)

def low_pass(kept, grad):
    return (grad,)

def back_keep(v):
    return (v, None)

def back_low(kept, grad):
    return (low(grad),)
low.defvjp(low_keep, low_pass)
low_back.defvjp(back_keep, back_low)

def lambda_start():
    return 0.8 - 0.6 * math.exp(-0.3 * (LAYER - 1))

def product(left, right):
    return jnp.dot(left, right, precision=PRECISE, preferred_element_type=jnp.float32)

def norm_rows(values, gain):
    return values * lax.rsqrt(lax.optimization_barrier(jnp.mean(values * values, axis=-1, keepdims=True)) + EPSILON) * gain

def rotate(values, cosine, sine_table):
    half_width = values.shape[-1] // 2
    lower_half = values[..., :half_width]
    upper_half = values[..., half_width:]
    return jnp.concatenate([lower_half * cosine - upper_half * sine_table, upper_half * cosine + lower_half * sine_table], axis=-1)

def positions(segment_ids):
    grouped = segment_ids.reshape(TOKENS // GROUP, GROUP)
    index_row = jnp.arange(GROUP, dtype=jnp.int32)

    def group_positions(seg_row):
        before = lax.optimization_barrier(jnp.sum((seg_row[None, :] < seg_row[:, None]).astype(jnp.int32), axis=1))
        return index_row - before
    return lax.map(group_positions, grouped).reshape(TOKENS)

def frequency():
    return ROPE_BASE ** (-(jnp.arange(HALF // 2, dtype=jnp.float32) * 2.0 / HALF))

def attend(queries, key_rows, values, segment_ids, lambda_value):
    scale = HALF ** (-0.5)
    key_index = jnp.arange(GROUP, dtype=jnp.int32)

    def one_block(block_id):
        group_id = block_id // N_CTX
        row_first = block_id * TOK_DEV
        group_first = group_id * GROUP
        query_blk = lax.dynamic_slice_in_dim(queries, row_first, TOK_DEV, 0)
        key_blk = lax.dynamic_slice_in_dim(key_rows, group_first, GROUP, 0)
        value_blk = lax.dynamic_slice_in_dim(values, group_first, GROUP, 0)
        query_seg = lax.dynamic_slice_in_dim(segment_ids, row_first, TOK_DEV, 0)
        key_seg = lax.dynamic_slice_in_dim(segment_ids, group_first, GROUP, 0)
        query_index = row_first - group_first + jnp.arange(TOK_DEV, dtype=jnp.int32)
        allowed = (query_seg[:, None] == key_seg[None, :]) & (key_index[None, :] <= query_index[:, None])
        score_one = low_back(jnp.einsum('thd,khd->htk', query_blk[:, :, 0], key_blk[:, :, 0], precision=PRECISE) * scale)
        score_two = low_back(jnp.einsum('thd,khd->htk', query_blk[:, :, 1], key_blk[:, :, 1], precision=PRECISE) * scale)
        prob_one = jax.nn.softmax(jnp.where(allowed[None], score_one, NEGATIVE), axis=-1)
        prob_two = jax.nn.softmax(jnp.where(allowed[None], score_two, NEGATIVE), axis=-1)
        out_one = low_back(jnp.einsum('htk,khd->thd', low(prob_one), value_blk, precision=PRECISE))
        out_two = low_back(jnp.einsum('htk,khd->thd', low(prob_two), value_blk, precision=PRECISE))
        return out_one - lambda_value * out_two
    blocks = jnp.arange(TOKENS // TOK_DEV, dtype=jnp.int32)
    return lax.map(jax.checkpoint(one_block), blocks).reshape(TOKENS, H, VD)

def forward(tokens, gain_attn, w_query, w_key, w_value, w_output, lambda_vec, gain_heads, gain_ffn, w_gate, w_up, w_down, segment_ids=None, cosine=None, sine_table=None):
    lambda_init = lambda_start()
    normed_in = low(norm_rows(tokens, gain_attn))
    query_pre = low_back(product(normed_in, w_query)).reshape(TOKENS, H, 2, HALF)
    queries = low(rotate(query_pre, cosine, sine_table))
    key_pre = low_back(product(normed_in, w_key)).reshape(TOKENS, H, 2, HALF)
    key_rows = low(rotate(key_pre, cosine, sine_table))
    values = low(low_back(product(normed_in, w_value))).reshape(TOKENS, H, VD)
    lambda_value = jnp.exp(jnp.sum(lambda_vec[0] * lambda_vec[1])) - jnp.exp(jnp.sum(lambda_vec[2] * lambda_vec[3])) + lambda_init
    mixed = attend(queries, key_rows, values, segment_ids, lambda_value)
    head_out = low(norm_rows(mixed, gain_heads) * (1.0 - lambda_init)).reshape(TOKENS, H * VD)
    residual = tokens + low_back(product(head_out, w_output))
    normed_mid = low(norm_rows(residual, gain_ffn))
    gate_pre = low_back(product(normed_mid, w_gate))
    up_pre = low_back(product(normed_mid, w_up))
    hidden = low(jax.nn.silu(gate_pre) * up_pre)
    return residual + product(hidden, w_down)

def reference(tokens, segment_ids, gain_attn, w_query, w_key, w_value, w_output, lambda_vec, gain_heads, gain_ffn, w_gate, w_up, w_down, grad_out):
    angles = positions(segment_ids).astype(jnp.float32)[:, None] * frequency()[None, :]
    cosine = jnp.cos(angles)[:, None, None, :]
    sine_table = jnp.sin(angles)[:, None, None, :]
    layer_call = functools.partial(forward, segment_ids=segment_ids, cosine=cosine, sine_table=sine_table)
    primals = (tokens.astype(jnp.float32), gain_attn, w_query.astype(jnp.float32), w_key.astype(jnp.float32), w_value.astype(jnp.float32), w_output.astype(jnp.float32), lambda_vec, gain_heads, gain_ffn, w_gate.astype(jnp.float32), w_up.astype(jnp.float32), w_down.astype(jnp.float32))
    result, pullback = jax.vjp(layer_call, *primals)
    gradients = pullback(grad_out.astype(jnp.float32))
    return (result.astype(jnp.bfloat16), gradients[0], gradients[1], gradients[2], gradients[3], gradients[4], gradients[5], gradients[6], gradients[7], gradients[8], gradients[9], gradients[10], gradients[11])
```

```python
import functools
import math

import jax
import jax.numpy as jnp
from jax import lax
from jax.experimental import pallas as pl
from jax.experimental.pallas import tpu as pltpu
from jax.sharding import PartitionSpec as P

HALF = 64
VD = 128
LAYER = 6
EPSILON = 1e-06
ROPE_BASE = 10000.0
MAX_START = -1e30
MASKED = -2e38
SCALE = HALF ** (-0.5)
LAMBDA_START = 0.8 - 0.6 * math.exp(-0.3 * (LAYER - 1))
KEEP = 1.0 - LAMBDA_START

BF16 = jnp.bfloat16
F32 = jnp.float32
VMEM_LIMIT = 60 * 1024 * 1024


def shape(dims, dtype):
    return jax.ShapeDtypeStruct(tuple(dims), dtype)


def whole(memory=pltpu.VMEM):
    return pl.BlockSpec(memory_space=memory)


def fixed(dims):
    zeros = (0,) * len(dims)
    return pl.BlockSpec(tuple(dims), lambda *_: zeros)


def call(body, outs, ins, *, name, grid=None, in_specs=None, out_specs=None, scratch=(), flops=0, move=0):
    if in_specs is None:
        in_specs = [whole(pltpu.SMEM) if a.ndim == 1 and a.dtype == jnp.int32 else whole() for a in ins]
    if out_specs is None:
        out_specs = [whole() for _ in outs]
    kwargs = {}
    if grid is not None:
        kwargs["grid"] = grid
    if not move:
        move = sum(a.size * a.dtype.itemsize for a in list(ins) + list(outs))
    return pl.pallas_call(
        body,
        out_shape=list(outs),
        in_specs=in_specs,
        out_specs=out_specs,
        scratch_shapes=list(scratch),
        compiler_params=pltpu.CompilerParams(vmem_limit_bytes=VMEM_LIMIT),
        cost_estimate=pl.CostEstimate(flops=1, bytes_accessed=1, transcendentals=0),
        name=name,
        **kwargs,
    )(*ins)


def dot(left, right, left_dim, right_dim):
    return lax.dot_general(
        left, right, (((left_dim,), (right_dim,)), ((), ())), preferred_element_type=F32
    )


def xor_pairs(count, step):
    return [(i, i ^ step) for i in range(count)]


def head_move(value, step):
    return lax.ppermute(value, "head", xor_pairs(lax.axis_size("head"), step))


def core_swap(value):
    return lax.ppermute(value, "dp", xor_pairs(lax.axis_size("dp"), 1))


def head_gather(unit):
    return [unit] + [head_move(unit, k) for k in range(1, lax.axis_size("head"))]


def after(value, *others):
    return lax.optimization_barrier((value,) + others)[0]


def place_rows(units, places, count):
    rows, cols = units[0].shape

    def body(at_ref, *refs):
        out = refs[-1]
        for i, ref in enumerate(refs[:-1]):
            start = pl.multiple_of(at_ref[i] * rows, 16)
            out[pl.ds(start, rows), :] = ref[...]

    return call(
        body, [shape((rows * count, cols), units[0].dtype)], [places] + list(units), name="place_rows"
    )[0]


def gather_rows(unit):
    return lax.all_gather(unit, ("dp", "ctx"), axis=0, tiled=True)


def scatter_rows(sums):
    return lax.psum_scatter(sums, "ctx", scatter_dimension=0, tiled=True)


def all_sum(value):
    value = value + core_swap(value)
    step = 1
    while step < lax.axis_size("head"):
        value = value + head_move(value, step)
        step *= 2
    step = 1
    while step < lax.axis_size("ctx"):
        value = value + lax.ppermute(value, "ctx", xor_pairs(lax.axis_size("ctx"), step))
        step *= 2
    return value


def head_sum(value):
    step = 1
    while step < lax.axis_size("head"):
        value = value + head_move(value, step)
        step *= 2
    return value


def turn(value, cosine, sine, sign):
    groups = []
    lanes = lax.broadcasted_iota(jnp.int32, cosine.shape, 1)
    lower = lanes % HALF < HALF // 2
    for i in range(value.shape[1] // 128):
        part = value[:, i * 128 : (i + 1) * 128]
        swapped = jnp.where(
            lower, pltpu.roll(part, 128 - HALF // 2, axis=1), pltpu.roll(part, HALF // 2, axis=1)
        )
        groups.append(part * cosine + sign * (swapped * sine))
    return jnp.concatenate(groups, axis=1)


def half_lanes(value):
    lanes = lax.broadcasted_iota(jnp.int32, value.shape, 1)
    zero = jnp.zeros_like(value)
    return jnp.where(lanes < HALF, value, zero), jnp.where(lanes < HALF, zero, value)


def norm_project_kernel(units, gain, spot, weight, cosine, sine):
    rows, cols = units[0].shape
    count = len(units)
    width = weight.shape[1]
    tile = 256

    def body(spot_ref, gain_ref, weight_ref, cos_ref, sin_ref, *refs):
        ins, (x_ref, normed_ref, inv_ref, kv_ref) = refs[:count], refs[count:]
        total = jnp.zeros((tile, 1), F32)
        for ref in ins:
            v = ref[...].astype(F32)
            total = total + jnp.sum(v * v, axis=1, keepdims=True)
        inv = lax.rsqrt(total / (count * cols) + EPSILON)
        inv_ref[...] = inv
        for k, ref in enumerate(ins):
            at = pl.ds(pl.multiple_of((spot_ref[0] ^ k) * cols, 128), cols)
            v = ref[...]
            x_ref[:, at] = v
            normed_ref[:, at] = (v.astype(F32) * inv * gain_ref[:, at]).astype(BF16)
        y = dot(normed_ref[...], weight_ref[...], 1, 0)
        for h in range(width // (2 * VD)):
            at = 2 * h * VD
            turned = turn(y[:, at : at + VD], cos_ref[...], sin_ref[...], 1.0)
            kv_ref[:, at : at + VD] = turned.astype(BF16)
            kv_ref[:, at + VD : at + 2 * VD] = y[:, at + VD : at + 2 * VD].astype(BF16)

    def tall(w):
        return pl.BlockSpec((tile, w), lambda i: (i, 0))

    wide = cols * count
    return call(
        body,
        [
            shape((rows, wide), BF16),
            shape((rows, wide), BF16),
            shape((rows, 1), F32),
            shape((rows, width), BF16),
        ],
        [spot, gain, weight, cosine, sine] + units,
        grid=(rows // tile,),
        in_specs=[whole(pltpu.SMEM), fixed(gain.shape), fixed(weight.shape), tall(128), tall(128)]
        + [tall(cols)] * count,
        out_specs=[tall(wide), tall(wide), tall(1), tall(width)],
        name="norm_project",
        flops=2 * rows * wide * width,
    )


def place_cols_kernel(units, spot):
    rows, cols = units[0].shape
    count = len(units)

    def body(spot_ref, *refs):
        for k, ref in enumerate(refs[:count]):
            at = pl.ds(pl.multiple_of((spot_ref[0] ^ k) * cols, 128), cols)
            refs[count][:, at] = ref[...]

    return call(body, [shape((rows, cols * count), BF16)], [spot] + units, name="place_cols")[0]


def query_kernel(x, weight, cols, cosine, sine):
    rows, wide = x.shape
    tile = 256

    def body(x_ref, weight_ref, cos_ref, sin_ref, out_ref):
        y = dot(x_ref[...], weight_ref[...], 1, 0)
        out_ref[...] = turn(y, cos_ref[...], sin_ref[...], 1.0).astype(BF16)

    def tall(width):
        return pl.BlockSpec((tile, width), lambda i: (i, 0))

    return call(
        body,
        [shape((rows, cols), BF16)],
        [x, weight, cosine, sine],
        grid=(rows // tile,),
        in_specs=[tall(wide), fixed((wide, cols)), tall(128), tall(128)],
        out_specs=[tall(cols)],
        name="queries",
        flops=2 * rows * wide * cols,
    )[0]


ATTN_TILE = 256


def tile_needed(meta_ref, slot, qi, ki, rows):
    key_last = (meta_ref[0] - slot) * rows + (ki + 1) * ATTN_TILE - 1
    return jnp.logical_and(meta_ref[0] >= slot, key_last >= meta_ref[1 + qi])


def score_mask(meta_ref, slot, qi, ki, rows, first):
    dims = (ATTN_TILE, ATTN_TILE)
    key_at = lax.broadcasted_iota(jnp.int32, dims, 0) + ((meta_ref[0] - slot) * rows + ki * ATTN_TILE)
    ok = key_at >= first
    if slot == 0 and qi == ki:
        query_at = lax.broadcasted_iota(jnp.int32, dims, 1) + (meta_ref[0] * rows + qi * ATTN_TILE)
        ok = jnp.logical_and(ok, key_at <= query_at)
    return ok


def attend_kernel(slot, first, last, meta, lam, q, kv, low, gain, state):
    rows = q.shape[0]
    heads = q.shape[1] // VD
    tile = ATTN_TILE
    tiles = rows // tile

    def body(meta_ref, lam_ref, q_ref, k_ref, v_ref, low_ref, gain_ref, *refs):
        if first:
            outs = refs
        else:
            acc_in, stat_in = refs[:2]
            outs = refs[2:]
        if last:
            head_ref, unit_ref, two_ref, fin_ref, acc, stat = outs
        else:
            acc, stat = outs
        if first:
            acc[...] = jnp.zeros_like(acc)
            stat[0:2, :] = jnp.full((2, rows), MAX_START, F32)
            stat[2:8, :] = jnp.zeros((6, rows), F32)
        else:
            acc[...] = acc_in[...]
            stat[...] = stat_in[...]
        for qi in range(tiles):
            cols = slice(qi * tile, (qi + 1) * tile)
            halves = half_lanes(q_ref[cols, :] * BF16(SCALE))
            for ki in range(tiles):
                if slot == 0 and ki > qi:
                    continue

                @pl.when(tile_needed(meta_ref, slot, qi, ki, rows))
                def _(qi=qi, ki=ki, cols=cols, halves=halves):
                    keys = k_ref[ki * tile : (ki + 1) * tile, :]
                    vals = v_ref[ki * tile : (ki + 1) * tile, :]
                    ok = score_mask(meta_ref, slot, qi, ki, rows, low_ref[0:1, cols])
                    for half in range(2):
                        score = jnp.where(ok, dot(keys, halves[half], 1, 1), MASKED)
                        old = stat[half : half + 1, cols]
                        new = jnp.maximum(old, jnp.max(score, axis=0, keepdims=True))
                        prob = jnp.exp(score - new)
                        fade = jnp.exp(old - new)
                        stat[half : half + 1, cols] = new
                        stat[2 + half : 3 + half, cols] = stat[2 + half : 3 + half, cols] * fade + jnp.sum(
                            prob, axis=0, keepdims=True
                        )
                        at = slice(half * VD, (half + 1) * VD)
                        acc[at, cols] = acc[at, cols] * fade + dot(vals, prob.astype(BF16), 0, 0)

        if last:
            out_one = acc[0:VD, :] / stat[2:3, :]
            out_two = acc[VD : 2 * VD, :] / stat[3:4, :]
            mixed = out_one - lam_ref[0, 0] * out_two
            inv = lax.rsqrt(jnp.mean(mixed * mixed, axis=0, keepdims=True) + EPSILON)
            unit = mixed * inv
            unit_ref[...] = unit
            two_ref[...] = out_two
            fin_ref[0:2, :] = stat[0:2, :] + jnp.log(stat[2:4, :])
            fin_ref[2:3, :] = inv
            fin_ref[3:8, :] = jnp.zeros((5, rows), F32)
            head_ref[...] = (jnp.transpose(unit) * gain_ref[...] * KEEP).astype(BF16)

    col = pl.BlockSpec((rows, VD), lambda h: (0, h))
    acc_spec = pl.BlockSpec((2 * VD, rows), lambda h: (h, 0))
    stat_spec = pl.BlockSpec((8, rows), lambda h: (h, 0))
    row_spec = pl.BlockSpec((VD, rows), lambda h: (h, 0))
    key_spec = pl.BlockSpec((rows, VD), lambda h: (0, 2 * h))
    value_spec = pl.BlockSpec((rows, VD), lambda h: (0, 2 * h + 1))
    in_specs = [whole(pltpu.SMEM), whole(pltpu.SMEM), col, key_spec, value_spec, fixed(low.shape), fixed(gain.shape)]
    ins = [meta, lam, q, kv, kv, low, gain]
    if not first:
        in_specs += [acc_spec, stat_spec]
        ins += list(state)
    outs, out_specs, scratch = [], [], []
    if last:
        outs = [
            shape((rows, heads * VD), BF16),
            shape((heads * VD, rows), F32),
            shape((heads * VD, rows), F32),
            shape((heads * 8, rows), F32),
        ]
        out_specs = [col, row_spec, row_spec, stat_spec]
        scratch = [pltpu.VMEM((2 * VD, rows), F32), pltpu.VMEM((8, rows), F32)]
    else:
        outs = [shape((heads * 2 * VD, rows), F32), shape((heads * 8, rows), F32)]
        out_specs = [acc_spec, stat_spec]
    return call(
        body,
        outs,
        ins,
        grid=(heads,),
        in_specs=in_specs,
        out_specs=out_specs,
        scratch=scratch,
        name=f"attend_{slot}",
        flops=2 * heads * rows * rows * (2 * HALF + 2 * VD),
    )


def attend_back_kernel(slot, meta, lam, q, kv, low, grad, stats, dq):
    rows = q.shape[0]
    heads = q.shape[1] // VD
    tile = ATTN_TILE
    tiles = rows // tile

    def body(meta_ref, lam_ref, q_ref, k_ref, v_ref, low_ref, grad_ref, stat_ref, *refs):
        if dq is not None:
            dq_in, dq_ref, dkv_ref, dk_acc, dv_acc = refs
            dq_ref[...] = dq_in[...]
        else:
            dq_ref, dkv_ref, dk_acc, dv_acc = refs
            dq_ref[...] = jnp.zeros_like(dq_ref)
        dk_acc[...] = jnp.zeros_like(dk_acc)
        dv_acc[...] = jnp.zeros_like(dv_acc)
        lam_value = lam_ref[0, 0]
        for qi in range(tiles):
            cols = slice(qi * tile, (qi + 1) * tile)
            q_one, q_two = half_lanes(q_ref[cols, :] * BF16(SCALE))
            for ki in range(tiles):
                if slot == 0 and ki > qi:
                    continue

                @pl.when(tile_needed(meta_ref, slot, qi, ki, rows))
                def _(qi=qi, ki=ki, cols=cols, q_one=q_one, q_two=q_two):
                    at = slice(ki * tile, (ki + 1) * tile)
                    keys = k_ref[at, :]
                    k_one, k_two = half_lanes(keys * BF16(SCALE))
                    grads = grad_ref[:, cols]
                    ok = score_mask(meta_ref, slot, qi, ki, rows, low_ref[0:1, cols])
                    inner = dot(v_ref[at, :], grads, 1, 0)
                    one = jnp.exp(jnp.where(ok, dot(keys, q_one, 1, 1), MASKED) - stat_ref[0:1, cols])
                    two = lam_value * jnp.exp(
                        jnp.where(ok, dot(keys, q_two, 1, 1), MASKED) - stat_ref[1:2, cols]
                    )
                    dv_acc[at, :] += dot((one - two).astype(BF16), grads, 1, 1)
                    d_one = (one * (inner - stat_ref[2:3, cols])).astype(BF16)
                    d_two = (two * (stat_ref[3:4, cols] - inner)).astype(BF16)
                    dk_acc[at, :] += dot(d_one, q_one, 1, 0) + dot(d_two, q_two, 1, 0)
                    dq_ref[cols, :] += dot(d_one, k_one, 0, 0) + dot(d_two, k_two, 0, 0)

        dkv_ref[:, :VD] = dk_acc[...].astype(BF16)
        dkv_ref[:, VD:] = dv_acc[...].astype(BF16)

    col = pl.BlockSpec((rows, VD), lambda h: (0, h))
    ins = [meta, lam, q, kv, kv, low, grad, stats]
    in_specs = [
        whole(pltpu.SMEM),
        whole(pltpu.SMEM),
        col,
        pl.BlockSpec((rows, VD), lambda h: (0, 2 * h)),
        pl.BlockSpec((rows, VD), lambda h: (0, 2 * h + 1)),
        fixed(low.shape),
        pl.BlockSpec((VD, rows), lambda h: (h, 0)),
        pl.BlockSpec((8, rows), lambda h: (h, 0)),
    ]
    if dq is not None:
        ins.append(dq)
        in_specs.append(col)
    return call(
        body,
        [shape((rows, heads * VD), F32), shape((rows, heads * 2 * VD), BF16)],
        ins,
        grid=(heads,),
        in_specs=in_specs,
        out_specs=[col, pl.BlockSpec((rows, 2 * VD), lambda h: (0, h))],
        scratch=[pltpu.VMEM((rows, VD), F32), pltpu.VMEM((rows, VD), F32)],
        name=f"attend_back_{slot}",
        flops=2 * heads * rows * rows * (4 * HALF + 2 * VD + 4 * HALF),
    )


def middle_kernel(x, heads_out, mine, theirs, gain, spot):
    rows, wide = x.shape
    half = wide // 2
    count = len(heads_out)
    cols = heads_out[0].shape[1]
    tile = 256

    def body(spot_ref, x_ref, gain_ref, *refs):
        ho, wm, wt = refs[:count], refs[count : 2 * count], refs[2 * count]
        resid_ref, normed_ref, inv_ref = refs[2 * count + 1 :]
        wt = [wt.at[k * half : (k + 1) * half, :] for k in range(count)]
        total = jnp.zeros((tile, 1), F32)
        for side, weights in ((0, wm), (1, wt)):
            at = pl.ds(pl.multiple_of((spot_ref[1] ^ side) * half, 128), half)
            value = x_ref[:, at].astype(F32)
            for k in range(count):
                value = value + dot(ho[k][...], weights[k][...], 1, 1)
            resid_ref[:, at] = value
            total = total + jnp.sum(value * value, axis=1, keepdims=True)
        inv = lax.rsqrt(total / wide + EPSILON)
        inv_ref[...] = inv
        normed_ref[...] = (resid_ref[...] * inv * gain_ref[...]).astype(BF16)

    def tall(width):
        return pl.BlockSpec((tile, width), lambda i: (i, 0))

    return call(
        body,
        [shape((rows, wide), F32), shape((rows, wide), BF16), shape((rows, 1), F32)],
        [spot, x, gain] + heads_out + mine + [theirs],
        grid=(rows // tile,),
        in_specs=[whole(pltpu.SMEM), tall(wide), fixed(gain.shape)]
        + [tall(cols)] * count
        + [fixed(mine[0].shape)] * count
        + [fixed(theirs.shape)],
        out_specs=[tall(wide), tall(wide), tall(1)],
        name="middle",
        flops=2 * rows * wide * cols * count,
    )


def gate_kernel(x, weight, first, cols):
    rows, wide = x.shape
    tile = 512 if cols % 512 == 0 and first % 512 == 0 else 256

    def body(x_ref, weight_ref, out_ref):
        out_ref[...] = dot(x_ref[...], weight_ref[...], 1, 0).astype(BF16)

    return call(
        body,
        [shape((rows, cols), BF16)],
        [x, weight],
        grid=(cols // tile,),
        in_specs=[fixed(x.shape), pl.BlockSpec((wide, tile), lambda i: (0, first // tile + i))],
        out_specs=[pl.BlockSpec((rows, tile), lambda i: (0, i))],
        name="gate",
    )[0]


def up_kernel(x, weight, first, gate):
    rows, wide = x.shape
    cols = gate.shape[1]
    tile = 512 if cols % 512 == 0 and first % 512 == 0 else 256

    def body(x_ref, weight_ref, gate_ref, up_ref, hidden_ref):
        up = dot(x_ref[...], weight_ref[...], 1, 0)
        up_ref[...] = up.astype(BF16)
        gate = gate_ref[...].astype(F32)
        hidden_ref[...] = (gate * jax.nn.sigmoid(gate) * up).astype(BF16)

    strip = pl.BlockSpec((rows, tile), lambda i: (0, i))
    return call(
        body,
        [shape((rows, cols), BF16), shape((rows, cols), BF16)],
        [x, weight, gate],
        grid=(cols // tile,),
        in_specs=[fixed(x.shape), pl.BlockSpec((wide, tile), lambda i: (0, first // tile + i)), strip],
        out_specs=[strip, strip],
        name="up",
    )


def gate_back_kernel(dy, weight, first, gate, up):
    rows, wide = dy.shape
    cols = gate.shape[1]
    tile = 512 if cols % 512 == 0 and first % 512 == 0 else 256

    def body(dy_ref, weight_ref, gate_ref, up_ref, dgate_ref, dup_ref):
        grad = dot(dy_ref[...], weight_ref[...], 1, 0)
        gate = gate_ref[...].astype(F32)
        sig = jax.nn.sigmoid(gate)
        dgate_ref[...] = (grad * up_ref[...].astype(F32) * sig * (1.0 + gate * (1.0 - sig))).astype(BF16)
        dup_ref[...] = (grad * gate * sig).astype(BF16)

    strip = pl.BlockSpec((rows, tile), lambda i: (0, i))
    return call(
        body,
        [shape((rows, cols), BF16), shape((rows, cols), BF16)],
        [dy, weight, gate, up],
        grid=(cols // tile,),
        in_specs=[
            fixed(dy.shape),
            pl.BlockSpec((wide, tile), lambda i: (0, first // tile + i)),
            strip,
            strip,
        ],
        out_specs=[strip, strip],
        name="gate_back",
    )


def quarters_kernel(terms, spot, count, name, norm=None):
    rows = terms[0][0].shape[0]
    wide = terms[0][1].shape[0]
    cols = wide // count
    n = len(terms)

    def body(spot_ref, *refs):
        lefts, weights = refs[:n], refs[n : 2 * n]
        rest = refs[2 * n :]
        if norm is not None:
            x_ref, inv_ref, gain_ref = rest[:3]
            rest = rest[3:]
            row_ref, col_ref = rest[count:]
        outs = rest[:count]
        pos = pl.program_id(0)
        value = dot(lefts[0][...], weights[0][...], 1, 1)
        for i in range(1, n):
            value = value + dot(lefts[i][...], weights[i][...], 1, 1)
        if norm is not None:
            weighed = value * (x_ref[...].astype(F32) * inv_ref[...])
            col_ref[...] = jnp.sum(weighed, axis=0, keepdims=True)
            row_sum = jnp.sum(weighed * gain_ref[...], axis=1, keepdims=True)

            @pl.when(pos == 0)
            def _():
                row_ref[...] = row_sum

            @pl.when(pos > 0)
            def _():
                row_ref[...] += row_sum

        value = value.astype(BF16)
        for k in range(count):

            @pl.when(spot_ref[0] ^ k == pos)
            def _(k=k):
                outs[k][...] = value

    ins = [spot] + [t[0] for t in terms] + [t[1] for t in terms]
    in_specs = [whole(pltpu.SMEM)] + [fixed(t[0].shape) for t in terms]
    for left, _, first in terms:
        width = left.shape[1]
        in_specs.append(pl.BlockSpec((cols, width), lambda i, at=first // width: (i, at)))
    outs = [shape((rows, cols), BF16)] * count
    out_specs = [fixed((rows, cols))] * count
    if norm is not None:
        ins += list(norm)
        in_specs += [
            pl.BlockSpec((rows, cols), lambda i: (0, i)),
            fixed((rows, 1)),
            pl.BlockSpec((1, cols), lambda i: (0, i)),
        ]
        outs = outs + [shape((rows, 1), F32), shape((1, wide), F32)]
        out_specs = out_specs + [fixed((rows, 1)), pl.BlockSpec((1, cols), lambda i: (0, i))]
    return call(body, outs, ins, grid=(count,), in_specs=in_specs, out_specs=out_specs, name=name)


def mid_back_kernel(dgate, dup, gate_w, gate_first, up_w, up_first, head_at, count):
    rows, cols = dgate.shape
    wide = gate_w.shape[0]
    tile = 384
    steps = wide // tile
    part = rows // count

    def body(at_ref, dgate_ref, dup_ref, g_ref, u_ref, *refs):
        outs = refs[:count]
        value = dot(dgate_ref[...], g_ref[...], 1, 1) + dot(dup_ref[...], u_ref[...], 1, 1)
        value = value.astype(BF16)
        for row in range(count):
            rows_of = value[row * part : (row + 1) * part, :]
            for k in range(count):

                @pl.when(at_ref[0] ^ k == row)
                def _(k=k, rows_of=rows_of):
                    outs[k][...] = rows_of

    return call(
        body,
        [shape((part, wide), BF16)] * count,
        [head_at, dgate, dup, gate_w, up_w],
        grid=(steps,),
        in_specs=[
            whole(pltpu.SMEM),
            fixed(dgate.shape),
            fixed(dup.shape),
            pl.BlockSpec((tile, cols), lambda i: (i, gate_first // cols)),
            pl.BlockSpec((tile, cols), lambda i: (i, up_first // cols)),
        ],
        out_specs=[pl.BlockSpec((part, tile), lambda i: (0, i))] * count,
        name="mid_back",
    )


def norm_mid_back_kernel(parts, resid, inv, gain, dy, spot):
    part, wide = parts[0].shape
    count = len(parts)

    def body(spot_ref, gain_ref, resid_ref, inv_ref, dy_ref, *refs):
        ins, (out_ref, col_ref) = refs[:count], refs[count:]
        grad = ins[0][...].astype(F32)
        for ref in ins[1:]:
            grad = grad + ref[...].astype(F32)
        inv_rows = inv_ref[...]
        unit = resid_ref[...] * inv_rows
        col_ref[...] = jnp.sum(grad * unit, axis=0, keepdims=True)
        e = grad * gain_ref[...]
        mean = jnp.sum(e * unit, axis=1, keepdims=True) / wide
        out_ref[...] = (dy_ref[...].astype(F32) + inv_rows * (e - unit * mean)).astype(BF16)

    def mine(width):
        return pl.BlockSpec((part, width), lambda i, spot_ref: (spot_ref[0], 0))

    def all_of(dims):
        return pl.BlockSpec(tuple(dims), lambda i, spot_ref: (0, 0))

    return pl.pallas_call(
        body,
        out_shape=[shape((part, wide), BF16), shape((1, wide), F32)],
        grid_spec=pltpu.PrefetchScalarGridSpec(
            num_scalar_prefetch=1,
            grid=(1,),
            in_specs=[all_of(gain.shape), mine(wide), mine(1), mine(wide)] + [all_of((part, wide))] * count,
            out_specs=[all_of((part, wide)), all_of((1, wide))],
        ),
        compiler_params=pltpu.CompilerParams(vmem_limit_bytes=VMEM_LIMIT),
        cost_estimate=pl.CostEstimate(flops=1, bytes_accessed=1, transcendentals=0),
        name="norm_mid_back",
    )(spot, gain, resid, inv, dy, *parts)


def head_back_kernel(branch, weight, first, cols, unit, two, fin, gain, lam):
    rows, wide = branch.shape
    heads = cols // VD

    def body(lam_ref, b_ref, weight_ref, unit_ref, two_ref, fin_ref, gain_ref, g_ref, stat_ref, sum_ref):
        grad = jnp.transpose(dot(b_ref[...], weight_ref[...], 1, 0))
        unit = unit_ref[...]
        out_two = two_ref[...]
        inv = fin_ref[2:3, :]
        f = grad * gain_ref[...] * KEEP
        mean = jnp.mean(f * unit, axis=0, keepdims=True)
        mixed_grad = inv * (f - unit * mean)
        g = mixed_grad.astype(BF16)
        g_ref[...] = g
        g = g.astype(F32)
        delta_two = jnp.sum(g * out_two, axis=0, keepdims=True)
        mixed = unit / inv
        stat_ref[0:2, :] = fin_ref[0:2, :]
        stat_ref[2:3, :] = jnp.sum(g * mixed, axis=0, keepdims=True) + lam_ref[0, 0] * delta_two
        stat_ref[3:4, :] = delta_two
        stat_ref[4:8, :] = jnp.zeros((4, rows), F32)
        gain_term = jnp.sum(grad * unit, axis=1, keepdims=True) * KEEP
        lam_term = -jnp.sum(mixed_grad * out_two, axis=1, keepdims=True)
        lanes = lax.broadcasted_iota(jnp.int32, (VD, 128), 1)
        sum_ref[...] = jnp.where(lanes == 0, gain_term, jnp.where(lanes == 1, lam_term, 0.0))

    row_spec = pl.BlockSpec((VD, rows), lambda h: (h, 0))
    stat_spec = pl.BlockSpec((8, rows), lambda h: (h, 0))
    slab = pl.BlockSpec((wide, VD), lambda h: (0, first // VD + h))
    return call(
        body,
        [shape((cols, rows), BF16), shape((heads * 8, rows), F32), shape((heads * VD, 128), F32)],
        [lam, branch, weight, unit, two, fin, gain],
        grid=(heads,),
        in_specs=[
            whole(pltpu.SMEM),
            fixed(branch.shape),
            slab,
            row_spec,
            row_spec,
            stat_spec,
            fixed(gain.shape),
        ],
        out_specs=[row_spec, stat_spec, pl.BlockSpec((VD, 128), lambda h: (h, 0))],
        name="head_back",
        flops=2 * rows * wide * cols,
    )


def turn_back_kernel(value, extra, cosine, sine, step, name):
    rows, cols = value.shape
    tile = 256
    with_extra = extra is not None

    def body(v_ref, *refs):
        v = v_ref[...].astype(F32)
        if with_extra:
            v = v + refs[0][...].astype(F32)
        cos_ref, sin_ref, out_ref = refs[-3:]
        for at in range(0, cols, 128):
            part = v[:, at : at + 128]
            if at % step == 0:
                part = turn(part, cos_ref[...], sin_ref[...], -1.0)
            out_ref[:, at : at + 128] = part.astype(BF16)

    def tall(width):
        return pl.BlockSpec((tile, width), lambda i: (i, 0))

    ins = [value] + ([extra] if with_extra else []) + [cosine, sine]
    return call(
        body,
        [shape((rows, cols), BF16)],
        ins,
        grid=(rows // tile,),
        in_specs=[tall(cols)] * (len(ins) - 2) + [tall(128), tall(128)],
        out_specs=[tall(cols)],
        name=name,
    )[0]


def outer_kernel(pairs, side, got, name):
    rows = pairs[0][0].shape[0]
    half = pairs[0][0].shape[1] // 2
    widths = [right.shape[1] for _, right in pairs]
    tile = 512 if all(w % 512 == 0 for w in widths) else 384
    steps = [w // tile for w in widths]
    starts = [sum(steps[:i]) for i in range(len(steps))]
    n = len(pairs)
    lefts = []
    for left, _ in pairs:
        if not any(left is other for other in lefts):
            lefts.append(left)
    left_of = [next(i for i, other in enumerate(lefts) if other is left) for left, _ in pairs]
    with_got = got is not None

    def body(side_ref, *refs):
        left_refs, right_refs = refs[: len(lefts)], refs[len(lefts) : len(lefts) + n]
        out_ref, turned = refs[-2:]
        step = pl.program_id(0)
        for i in range(n):
            if i == 0 or left_of[i] != left_of[i - 1]:

                @pl.when(step == starts[i])
                def _(i=i):
                    turned[...] = jnp.transpose(left_refs[left_of[i]][...])

            @pl.when(jnp.logical_and(step >= starts[i], step < starts[i] + steps[i]))
            def _(i=i):
                value = dot(turned[...], right_refs[i][...], 1, 0)
                if with_got:
                    value = value + refs[-3][...].astype(F32)
                out_ref[...] = value.astype(BF16)

    def right_spec(i):
        return pl.BlockSpec((rows, tile), lambda j, side_ref: (0, jnp.clip(j - starts[i], 0, steps[i] - 1)))

    strip = pl.BlockSpec((half, tile), lambda j, side_ref: (0, j))
    return pl.pallas_call(
        body,
        out_shape=shape((half, sum(widths)), BF16),
        grid_spec=pltpu.PrefetchScalarGridSpec(
            num_scalar_prefetch=1,
            grid=(sum(steps),),
            in_specs=[pl.BlockSpec((rows, half), lambda j, side_ref: (0, side_ref[0]))] * len(lefts)
            + [right_spec(i) for i in range(n)]
            + ([strip] if with_got else []),
            out_specs=strip,
            scratch_shapes=[pltpu.VMEM((half, rows), BF16)],
        ),
        compiler_params=pltpu.CompilerParams(vmem_limit_bytes=VMEM_LIMIT),
        cost_estimate=pl.CostEstimate(flops=1, bytes_accessed=1, transcendentals=0),
        name=name,
    )(side, *lefts, *[right for _, right in pairs], *([got] if with_got else []))


def per_device(
    tokens,
    segment_ids,
    gain_attn,
    w_query,
    w_key,
    w_value,
    w_output,
    lambda_vec,
    gain_heads,
    gain_ffn,
    w_gate,
    w_up,
    w_down,
    grad_out,
):
    rows, slice_width = tokens.shape
    n_ctx = lax.axis_size("ctx")
    n_head = lax.axis_size("head")
    place = lax.axis_index("ctx")
    head = lax.axis_index("head")
    core = lax.axis_index("dp")
    group = segment_ids.shape[0]
    wide = slice_width * n_head
    cols = w_query.shape[1]
    heads = cols // VD
    spot = jnp.stack([head, core]).astype(jnp.int32)
    my_side = jnp.reshape(core, (1,)).astype(jnp.int32)
    other_side = 1 - my_side
    reach = n_ctx
    if n_ctx == 4 and group == 3072 and rows == 768:
        reach = n_ctx - 1

    pieces = []
    for h in range(heads):
        pieces += [w_key[:, h * VD : (h + 1) * VD], w_value[:, h * VD : (h + 1) * VD]]
    kv_w = gather_rows(jnp.concatenate(pieces, axis=1))
    x_units = head_gather(tokens)
    hidden_cols = w_gate.shape[1]
    qo_w = gather_rows(jnp.concatenate([w_query, w_output.T], axis=1))
    g_w = gather_rows(w_gate)
    ud_w = gather_rows(jnp.concatenate([w_up, w_down.T], axis=1))

    first_row = place * rows
    row_index = first_row + jnp.arange(rows, dtype=jnp.int32)
    my_seg = lax.dynamic_slice_in_dim(segment_ids, first_row, rows, 0)
    before = jnp.sum((segment_ids[None, :] < my_seg[:, None]).astype(jnp.int32), axis=1)
    lane = jnp.arange(128, dtype=jnp.int32)
    frequency = ROPE_BASE ** (-((lane % (HALF // 2)).astype(F32) * 2.0 / HALF))
    angles = (row_index - before).astype(F32)[:, None] * frequency[None, :]
    cosine = jnp.cos(angles)
    sine = jnp.sin(angles) * jnp.where(lane % HALF < HALF // 2, -1.0, 1.0)[None, :]
    low = jnp.broadcast_to(before[None, :], (8, rows))
    meta = jnp.concatenate([jnp.reshape(place, (1,)), before[::ATTN_TILE]]).astype(jnp.int32)
    exp_one = jnp.exp(jnp.sum(lambda_vec[0] * lambda_vec[1]))
    exp_two = jnp.exp(jnp.sum(lambda_vec[2] * lambda_vec[3]))
    lam = jnp.reshape(exp_one - exp_two + LAMBDA_START, (1, 1))

    gain_in = gain_attn[None, :]
    gain_mid = gain_ffn[None, :]

    x_full, normed_in, inv_in, kv = norm_project_kernel(x_units, gain_in, spot, kv_w, cosine, sine)
    forward_pairs = [(i, i + 1) for i in range(n_ctx - 1)]
    kv_slots = [kv]
    kv_slots.append(lax.ppermute(kv, "ctx", forward_pairs))
    queries = query_kernel(normed_in, qo_w, cols, cosine, sine)
    o_half = lax.dynamic_slice(qo_w, (core * (wide // 2), cols), (wide // 2, cols))
    o_units = head_gather(after(o_half, queries))

    def attend(slot, state, kv_slot):
        return attend_kernel(
            slot, slot == 0, slot == reach - 1, meta, lam, queries, kv_slot, low, gain_heads[None, :], state
        )

    state = attend(0, None, kv)
    for slot in range(1, reach):
        here = after(kv_slots[slot], state[1])
        if slot + 1 < reach:
            kv_slots.append(lax.ppermute(here, "ctx", forward_pairs[slot:]))
        state = attend(slot, state, here)
    head_out, unit_head, out_two, finish = state
    ho_units = head_gather(head_out)
    o_theirs = core_swap(jnp.concatenate([after(o_units[0], head_out)] + o_units[1:], axis=0))
    dy_units = head_gather(after(grad_out, o_theirs))
    resid, normed_mid, inv_mid = middle_kernel(x_full, ho_units, o_units, o_theirs, gain_mid, spot)
    gate = gate_kernel(normed_mid, g_w, 0, hidden_cols)
    up, hidden = up_kernel(normed_mid, ud_w, 0, gate)
    dy = place_cols_kernel(dy_units, after(spot, hidden))
    dgate, dup = gate_back_kernel(dy, ud_w, hidden_cols, gate, up)
    mid_parts = mid_back_kernel(dgate, dup, g_w, 0, ud_w, 0, spot, n_head)
    mid_got = [head_move(mid_parts[k], k) for k in range(1, n_head)]

    ffn_pairs = [(dy, hidden), (normed_mid, dgate), (normed_mid, dup)]
    ffn_theirs = outer_kernel(ffn_pairs, after(other_side, mid_parts[0]), None, "ffn_grads_theirs")
    ffn_got = core_swap(ffn_theirs)
    y_parts = quarters_kernel([(hidden, ud_w, hidden_cols)], after(spot, ffn_theirs), n_head, "down")
    ffn_sums = outer_kernel(ffn_pairs, after(my_side, y_parts[0]), ffn_got, "ffn_grads")
    ffn_total = scatter_rows(ffn_sums)
    mid_got[0] = after(mid_got[0], ffn_sums)
    branch_rows, ffn_gain_term = norm_mid_back_kernel(
        [mid_parts[0]] + mid_got, resid, inv_mid, gain_mid, dy, spot
    )
    branch_units = head_gather(branch_rows)
    branch = place_rows(
        branch_units, jnp.stack([head ^ k for k in range(n_head)]).astype(jnp.int32), n_head
    )
    y_got = [head_move(after(y_parts[k], branch), k) for k in range(1, n_head)]

    grads, stats, head_sums = head_back_kernel(
        branch, qo_w, cols, cols, unit_head, out_two, finish, gain_heads[:, None], lam
    )
    dq = None
    dkv_got = None
    for slot in reversed(range(reach)):
        dq, dkv = attend_back_kernel(slot, meta, lam, queries, kv_slots[slot], low, grads, stats, dq)
        if slot:
            if dkv_got is not None:
                dkv = (after(dkv, dq).astype(F32) + dkv_got.astype(F32)).astype(BF16)
            dkv_got = lax.ppermute(dkv, "ctx", [(i, i - 1) for i in range(slot, n_ctx)])

    my_cols = head * slice_width
    output = lax.dynamic_slice_in_dim(resid, my_cols, slice_width, 1) + after(y_parts[0], dq).astype(F32)
    for got in y_got:
        output = output + got.astype(F32)
    output = output.astype(BF16)
    dq_pre = turn_back_kernel(after(dq, output), None, cosine, sine, VD, "query_back")
    oq_pairs = [(branch, head_out), (normed_in, dq_pre)]
    oq_theirs = outer_kernel(oq_pairs, other_side, None, "oq_grads_theirs")
    oq_got = core_swap(oq_theirs)
    oq_sums = outer_kernel(oq_pairs, after(my_side, oq_theirs), oq_got, "oq_grads")
    oq_total = scatter_rows(after(oq_sums, ffn_total))

    dkv_pre = turn_back_kernel(after(dkv, oq_sums), dkv_got, cosine, sine, 2 * VD, "key_back")
    kv_pairs = [(normed_in, dkv_pre)]
    kv_theirs = outer_kernel(kv_pairs, other_side, None, "kv_grads_theirs")
    kv_got = core_swap(kv_theirs)
    in_parts = quarters_kernel(
        [(dq_pre, qo_w, 0), (dkv_pre, kv_w, 0)],
        after(spot, kv_theirs),
        n_head,
        "in_back",
        norm=(x_full, inv_in, gain_in),
    )
    in_got = [head_move(in_parts[k], k) for k in range(1, n_head)]
    kv_sums = outer_kernel(kv_pairs, after(my_side, in_parts[0]), kv_got, "kv_grads")
    kv_total = scatter_rows(after(kv_sums, oq_total))
    row_sums, attn_gain_term = in_parts[n_head:]
    row_sums = head_sum(row_sums.reshape(rows // 128, 128)).reshape(rows, 1)
    grad_in = in_parts[0].astype(F32)
    for got in in_got:
        grad_in = grad_in + got.astype(F32)
    my_gain = lax.dynamic_slice_in_dim(gain_in, my_cols, slice_width, 1)
    my_branch = lax.dynamic_slice_in_dim(branch, my_cols, slice_width, 1).astype(F32)
    unit_in = tokens.astype(F32) * inv_in
    grad_tokens = my_branch + inv_in * (grad_in * my_gain - unit_in * (row_sums / wide))

    head_sums = jnp.sum(head_sums.reshape(heads, VD, 128), axis=0)
    small = jnp.concatenate(
        [
            attn_gain_term[0],
            ffn_gain_term[0],
            head_sums[:, 0],
            jnp.full((128,), jnp.sum(head_sums[:, 1]), F32),
        ]
    ).reshape(-1, 128)
    small = all_sum(small).reshape(-1)
    attn_gain_grad = small[:wide]
    ffn_gain_grad = small[wide : 2 * wide]
    heads_gain_grad = small[2 * wide : 2 * wide + VD]
    lambda_scalar = small[2 * wide + VD]
    grad_lambda = jnp.stack(
        [
            lambda_scalar * exp_one * lambda_vec[1],
            lambda_scalar * exp_one * lambda_vec[0],
            -lambda_scalar * exp_two * lambda_vec[3],
            -lambda_scalar * exp_two * lambda_vec[2],
        ],
        axis=0,
    )
    grad_kv = kv_total.astype(F32)
    grad_key = jnp.concatenate([grad_kv[:, 2 * h * VD : (2 * h + 1) * VD] for h in range(heads)], axis=1)
    grad_value = jnp.concatenate(
        [grad_kv[:, (2 * h + 1) * VD : (2 * h + 2) * VD] for h in range(heads)], axis=1
    )
    return (
        output,
        grad_tokens,
        attn_gain_grad,
        oq_total[:, cols:].astype(F32),
        grad_key,
        grad_value,
        oq_total[:, :cols].astype(F32).T,
        grad_lambda,
        heads_gain_grad,
        ffn_gain_grad,
        ffn_total[:, hidden_cols : 2 * hidden_cols].astype(F32),
        ffn_total[:, 2 * hidden_cols :].astype(F32),
        ffn_total[:, :hidden_cols].astype(F32).T,
    )


def solution(mesh):
    split = P(("dp", "ctx"), "head")
    turned = P("head", ("dp", "ctx"))
    in_specs = (
        split,
        P("dp"),
        P(),
        split,
        split,
        split,
        turned,
        P(),
        P(),
        P(),
        split,
        split,
        turned,
        split,
    )
    out_specs = (
        split,
        split,
        P(),
        split,
        split,
        split,
        turned,
        P(),
        P(),
        P(),
        split,
        split,
        turned,
    )
    return jax.shard_map(
        per_device, mesh=mesh, in_specs=in_specs, out_specs=out_specs, check_vma=False
    )
```

```python
import functools
import math

import jax
import jax.numpy as jnp
from jax import lax
from jax.experimental import pallas as pl
from jax.experimental.pallas import tpu as pltpu
from jax.sharding import PartitionSpec as P

HALF = 64
VD = 128
LAYER = 6
EPSILON = 1e-06
ROPE_BASE = 10000.0
MAX_START = -1e30
MASKED = -2e38
SCALE = HALF ** (-0.5)
LAMBDA_START = 0.8 - 0.6 * math.exp(-0.3 * (LAYER - 1))
KEEP = 1.0 - LAMBDA_START

BF16 = jnp.bfloat16
F32 = jnp.float32
VMEM_LIMIT = 60 * 1024 * 1024


LONG = {"place_rows": 1000, "norm_mid_back": 1000, "down": 1000}


def work(name):
    return pl.CostEstimate(flops=LONG.get(name, 0) * 10**9 + 1, bytes_accessed=1, transcendentals=0)


def shape(dims, dtype):
    return jax.ShapeDtypeStruct(tuple(dims), dtype)


def whole(memory=pltpu.VMEM):
    return pl.BlockSpec(memory_space=memory)


def fixed(dims):
    zeros = (0,) * len(dims)
    return pl.BlockSpec(tuple(dims), lambda *_: zeros)


def call(body, outs, ins, *, name, grid=None, in_specs=None, out_specs=None, scratch=(), flops=0, move=0):
    if in_specs is None:
        in_specs = [whole(pltpu.SMEM) if a.ndim == 1 and a.dtype == jnp.int32 else whole() for a in ins]
    if out_specs is None:
        out_specs = [whole() for _ in outs]
    kwargs = {}
    if grid is not None:
        kwargs["grid"] = grid
    if not move:
        move = sum(a.size * a.dtype.itemsize for a in list(ins) + list(outs))
    return pl.pallas_call(
        body,
        out_shape=list(outs),
        in_specs=in_specs,
        out_specs=out_specs,
        scratch_shapes=list(scratch),
        compiler_params=pltpu.CompilerParams(vmem_limit_bytes=VMEM_LIMIT),
        cost_estimate=work(name),
        name=name,
        **kwargs,
    )(*ins)


def dot(left, right, left_dim, right_dim):
    return lax.dot_general(
        left, right, (((left_dim,), (right_dim,)), ((), ())), preferred_element_type=F32
    )


def xor_pairs(count, step):
    return [(i, i ^ step) for i in range(count)]


def head_move(value, step):
    return lax.ppermute(value, "head", xor_pairs(lax.axis_size("head"), step))


def core_swap(value):
    return lax.ppermute(value, "dp", xor_pairs(lax.axis_size("dp"), 1))


def head_gather(unit):
    return [unit] + [head_move(unit, k) for k in range(1, lax.axis_size("head"))]


def after(value, *others):
    return lax.optimization_barrier((value,) + others)[0]


def place_rows(units, places, count):
    rows, cols = units[0].shape

    def body(at_ref, *refs):
        out = refs[-1]
        for i, ref in enumerate(refs[:-1]):
            start = pl.multiple_of(at_ref[i] * rows, 16)
            out[pl.ds(start, rows), :] = ref[...]

    return call(
        body, [shape((rows * count, cols), units[0].dtype)], [places] + list(units), name="place_rows"
    )[0]


def gather_rows(unit):
    return lax.all_gather(unit, ("dp", "ctx"), axis=0, tiled=True)


def scatter_rows(sums):
    return lax.psum_scatter(sums, "ctx", scatter_dimension=0, tiled=True)


def line_sum(value):
    value = value + core_swap(value)
    step = 1
    while step < lax.axis_size("ctx"):
        value = value + lax.ppermute(value, "ctx", xor_pairs(lax.axis_size("ctx"), step))
        step *= 2
    return value


def head_sum(value):
    step = 1
    while step < lax.axis_size("head"):
        value = value + head_move(value, step)
        step *= 2
    return value


def turn(value, cosine, sine, sign):
    groups = []
    lanes = lax.broadcasted_iota(jnp.int32, cosine.shape, 1)
    lower = lanes % HALF < HALF // 2
    for i in range(value.shape[1] // 128):
        part = value[:, i * 128 : (i + 1) * 128]
        swapped = jnp.where(
            lower, pltpu.roll(part, 128 - HALF // 2, axis=1), pltpu.roll(part, HALF // 2, axis=1)
        )
        groups.append(part * cosine + sign * (swapped * sine))
    return jnp.concatenate(groups, axis=1)


def half_lanes(value):
    lanes = lax.broadcasted_iota(jnp.int32, value.shape, 1)
    zero = jnp.zeros_like(value)
    return jnp.where(lanes < HALF, value, zero), jnp.where(lanes < HALF, zero, value)


def pack_kernel(keys, values, *others):
    rows, cols = keys.shape
    heads = cols // VD

    def body(k_ref, v_ref, *refs):
        out = refs[-1]
        for h in range(heads):
            at = 2 * h * VD
            out[:, at : at + VD] = k_ref[:, h * VD : (h + 1) * VD]
            out[:, at + VD : at + 2 * VD] = v_ref[:, h * VD : (h + 1) * VD]
        at = 2 * cols
        for ref in refs[:-1]:
            out[:, at : at + ref.shape[1]] = ref[...]
            at += ref.shape[1]

    width = 2 * cols + sum(other.shape[1] for other in others)
    return call(body, [shape((rows, width), keys.dtype)], [keys, values, *others], name="pack")[0]


def norm_in_kernel(units, gain, spot, keep):
    rows, cols = units[0].shape
    count = len(units)
    wide = cols * count
    tile = 256

    def body(spot_ref, gain_ref, *refs):
        ins, outs = refs[:count], refs[count:]
        total = jnp.zeros((tile, 1), F32)
        for ref in ins:
            v = ref[...].astype(F32)
            total = total + jnp.sum(v * v, axis=1, keepdims=True)
        inv = lax.rsqrt(total / wide + EPSILON)
        for k, ref in enumerate(ins):
            at = pl.ds(pl.multiple_of((spot_ref[0] ^ k) * cols, 128), cols)
            v = ref[...]
            outs[0][:, at] = (v.astype(F32) * inv * gain_ref[:, at]).astype(BF16)
            if keep:
                outs[1][:, at] = v
        if keep:
            outs[2][...] = inv

    def tall(w):
        return pl.BlockSpec((tile, w), lambda i: (i, 0))

    outs, out_specs = [shape((rows, wide), BF16)], [tall(wide)]
    if keep:
        outs += [shape((rows, wide), BF16), shape((rows, 1), F32)]
        out_specs += [tall(wide), tall(1)]
    return call(
        body,
        outs,
        [spot, gain] + units,
        grid=(rows // tile,),
        in_specs=[whole(pltpu.SMEM), fixed(gain.shape)] + [tall(cols)] * count,
        out_specs=out_specs,
        name="norm_in",
    )


def project_kernel(x, weight, width, more, cosine, sine):
    rows, wide = x.shape
    tile = 256

    def body(x_ref, weight_ref, cos_ref, sin_ref, *outs):
        y = dot(x_ref[...], weight_ref[...], 1, 0)
        for h in range(width // (2 * VD)):
            at = 2 * h * VD
            outs[0][:, at : at + VD] = turn(y[:, at : at + VD], cos_ref[...], sin_ref[...], 1.0).astype(BF16)
            outs[0][:, at + VD : at + 2 * VD] = y[:, at + VD : at + 2 * VD].astype(BF16)
        if more:
            outs[1][...] = turn(y[:, width:], cos_ref[...], sin_ref[...], 1.0).astype(BF16)

    def tall(w):
        return pl.BlockSpec((tile, w), lambda i: (i, 0))

    widths = [width] + ([more] if more else [])
    return call(
        body,
        [shape((rows, w), BF16) for w in widths],
        [x, weight, cosine, sine],
        grid=(rows // tile,),
        in_specs=[tall(wide), fixed((wide, width + more)), tall(128), tall(128)],
        out_specs=[tall(w) for w in widths],
        name="project",
    )


def place_cols_kernel(units, spot):
    rows, cols = units[0].shape
    count = len(units)

    def body(spot_ref, *refs):
        for k, ref in enumerate(refs[:count]):
            at = pl.ds(pl.multiple_of((spot_ref[0] ^ k) * cols, 128), cols)
            refs[count][:, at] = ref[...]

    return call(body, [shape((rows, cols * count), BF16)], [spot] + units, name="place_cols")[0]


ATTN_TILE = 384


def spans(meta_ref, slot, qi, rows):
    base = (meta_ref[0] - slot) * rows
    first = meta_ref[1 + qi]
    end = (qi + 1) * ATTN_TILE if slot == 0 else rows
    later = end - ATTN_TILE
    present = meta_ref[0] >= slot
    if later == 0:
        return [(slice(0, end), jnp.logical_and(present, first < base + end))]
    return [
        (slice(0, end), jnp.logical_and(present, first < base + later)),
        (
            slice(later, end),
            jnp.logical_and(present, jnp.logical_and(first >= base + later, first < base + end)),
        ),
    ]


def score_mask(meta_ref, slot, qi, at, rows, first):
    dims = (at.stop - at.start, ATTN_TILE)
    key_at = lax.broadcasted_iota(jnp.int32, dims, 0) + ((meta_ref[0] - slot) * rows + at.start)
    ok = key_at >= first
    if slot == 0:
        query_at = lax.broadcasted_iota(jnp.int32, dims, 1) + (meta_ref[0] * rows + qi * ATTN_TILE)
        ok = jnp.logical_and(ok, key_at <= query_at)
    return ok


def attend_kernel(slot, first, last, meta, lam, q, kv, low, gain, state):
    rows = q.shape[0]
    heads = q.shape[1] // VD
    tile = ATTN_TILE
    tiles = rows // tile

    def body(meta_ref, lam_ref, q_ref, k_ref, v_ref, low_ref, gain_ref, *refs):
        if first:
            outs = refs
        else:
            acc_in, stat_in = refs[:2]
            outs = refs[2:]
        if last:
            head_ref, unit_ref, two_ref, fin_ref, acc, stat = outs
        else:
            acc, stat = outs
        if first:
            acc[...] = jnp.zeros_like(acc)
            stat[0:2, :] = jnp.full((2, rows), MAX_START, F32)
            stat[2:8, :] = jnp.zeros((6, rows), F32)
        else:
            acc[...] = acc_in[...]
            stat[...] = stat_in[...]
        for qi in range(tiles):
            cols = slice(qi * tile, (qi + 1) * tile)
            halves = half_lanes(q_ref[cols, :] * BF16(SCALE))
            for at, needed in spans(meta_ref, slot, qi, rows):

                @pl.when(needed)
                def _(qi=qi, at=at, cols=cols, halves=halves):
                    keys = k_ref[at, :]
                    vals = v_ref[at, :]
                    ok = score_mask(meta_ref, slot, qi, at, rows, low_ref[0:1, cols])
                    for half in range(2):
                        score = jnp.where(ok, dot(keys, halves[half], 1, 1), MASKED)
                        old = stat[half : half + 1, cols]
                        new = jnp.maximum(old, jnp.max(score, axis=0, keepdims=True))
                        prob = jnp.exp(score - new)
                        fade = jnp.exp(old - new)
                        stat[half : half + 1, cols] = new
                        stat[2 + half : 3 + half, cols] = stat[2 + half : 3 + half, cols] * fade + jnp.sum(
                            prob, axis=0, keepdims=True
                        )
                        to = slice(half * VD, (half + 1) * VD)
                        acc[to, cols] = acc[to, cols] * fade + dot(vals, prob.astype(BF16), 0, 0)

        if last:
            out_one = acc[0:VD, :] / stat[2:3, :]
            out_two = acc[VD : 2 * VD, :] / stat[3:4, :]
            mixed = out_one - lam_ref[0, 0] * out_two
            inv = lax.rsqrt(jnp.mean(mixed * mixed, axis=0, keepdims=True) + EPSILON)
            unit = mixed * inv
            unit_ref[...] = unit
            two_ref[...] = out_two
            fin_ref[0:2, :] = stat[0:2, :] + jnp.log(stat[2:4, :])
            fin_ref[2:3, :] = inv
            fin_ref[3:8, :] = jnp.zeros((5, rows), F32)
            head_ref[...] = (jnp.transpose(unit) * gain_ref[...] * KEEP).astype(BF16)

    col = pl.BlockSpec((rows, VD), lambda h: (0, h))
    acc_spec = pl.BlockSpec((2 * VD, rows), lambda h: (h, 0))
    stat_spec = pl.BlockSpec((8, rows), lambda h: (h, 0))
    row_spec = pl.BlockSpec((VD, rows), lambda h: (h, 0))
    key_spec = pl.BlockSpec((rows, VD), lambda h: (0, 2 * h))
    value_spec = pl.BlockSpec((rows, VD), lambda h: (0, 2 * h + 1))
    in_specs = [whole(pltpu.SMEM), whole(pltpu.SMEM), col, key_spec, value_spec, fixed(low.shape), fixed(gain.shape)]
    ins = [meta, lam, q, kv, kv, low, gain]
    if not first:
        in_specs += [acc_spec, stat_spec]
        ins += list(state)
    outs, out_specs, scratch = [], [], []
    if last:
        outs = [
            shape((rows, heads * VD), BF16),
            shape((heads * VD, rows), F32),
            shape((heads * VD, rows), F32),
            shape((heads * 8, rows), F32),
        ]
        out_specs = [col, row_spec, row_spec, stat_spec]
        scratch = [pltpu.VMEM((2 * VD, rows), F32), pltpu.VMEM((8, rows), F32)]
    else:
        outs = [shape((heads * 2 * VD, rows), F32), shape((heads * 8, rows), F32)]
        out_specs = [acc_spec, stat_spec]
    return call(
        body,
        outs,
        ins,
        grid=(heads,),
        in_specs=in_specs,
        out_specs=out_specs,
        scratch=scratch,
        name=f"attend_{slot}",
        flops=2 * heads * rows * rows * (2 * HALF + 2 * VD),
    )


def attend_back_kernel(slot, finish, meta, lam, q, kv, low, grad, tables, sums):
    rows = q.shape[0]
    heads = q.shape[1] // VD
    want_q, want_k = sums[0] is not False, sums[1] is not False

    def body(meta_ref, lam_ref, q_ref, k_ref, v_ref, low_ref, grad_ref, cos_ref, sin_ref, *refs):
        refs = list(refs)
        dq_in = refs.pop(0) if want_q and sums[0] is not None else None
        dkv_in = refs.pop(0) if want_k and sums[1] is not None else None
        dq_out = refs.pop(0) if want_q else None
        dkv_out = refs.pop(0) if want_k else None
        dq_acc = refs.pop(0) if want_q else None
        if want_k:
            dk_acc, dv_acc = refs
        if want_q:
            dq_acc[...] = jnp.zeros_like(dq_acc) if dq_in is None else dq_in[...]
        if want_k:
            dk_acc[...] = jnp.zeros_like(dk_acc) if dkv_in is None else dkv_in[:, :VD]
            dv_acc[...] = jnp.zeros_like(dv_acc) if dkv_in is None else dkv_in[:, VD:]
        lam_value = lam_ref[0, 0]
        parts = grad_ref[VD : VD + 16, :].astype(F32)
        stat = parts[0:8, :] + parts[8:16, :]
        for qi in range(rows // ATTN_TILE):
            cols = slice(qi * ATTN_TILE, (qi + 1) * ATTN_TILE)
            q_one, q_two = half_lanes(q_ref[cols, :] * BF16(SCALE))
            for at, needed in spans(meta_ref, slot, qi, rows):

                @pl.when(needed)
                def _(qi=qi, at=at, cols=cols, q_one=q_one, q_two=q_two):
                    keys = k_ref[at, :]
                    grads = grad_ref[0:VD, cols]
                    ok = score_mask(meta_ref, slot, qi, at, rows, low_ref[0:1, cols])
                    inner = dot(v_ref[at, :], grads, 1, 0)
                    one = jnp.exp(jnp.where(ok, dot(keys, q_one, 1, 1), MASKED) - stat[0:1, cols])
                    two = lam_value * jnp.exp(
                        jnp.where(ok, dot(keys, q_two, 1, 1), MASKED) - stat[1:2, cols]
                    )
                    d_one = (one * (inner - stat[2:3, cols])).astype(BF16)
                    d_two = (two * (stat[3:4, cols] - inner)).astype(BF16)
                    if want_q:
                        k_one, k_two = half_lanes(keys * BF16(SCALE))
                        dq_acc[cols, :] += dot(d_one, k_one, 0, 0) + dot(d_two, k_two, 0, 0)
                    if want_k:
                        dv_acc[at, :] += dot((one - two).astype(BF16), grads, 1, 1)
                        dk_acc[at, :] += dot(d_one, q_one, 1, 0) + dot(d_two, q_two, 1, 0)

        if want_q:
            if finish[0]:
                dq_out[...] = turn(dq_acc[...], cos_ref[...], sin_ref[...], -1.0).astype(BF16)
            else:
                dq_out[...] = dq_acc[...]
        if want_k:
            if finish[1]:
                dkv_out[:, :VD] = turn(dk_acc[...], cos_ref[...], sin_ref[...], -1.0).astype(BF16)
                dkv_out[:, VD:] = dv_acc[...].astype(BF16)
            else:
                dkv_out[:, :VD] = dk_acc[...]
                dkv_out[:, VD:] = dv_acc[...]

    col = pl.BlockSpec((rows, VD), lambda h: (0, h))
    pair = pl.BlockSpec((rows, 2 * VD), lambda h: (0, h))
    ins = [meta, lam, q, kv, kv, low, grad, tables[0], tables[1]]
    in_specs = [
        whole(pltpu.SMEM),
        whole(pltpu.SMEM),
        col,
        pl.BlockSpec((rows, VD), lambda h: (0, 2 * h)),
        pl.BlockSpec((rows, VD), lambda h: (0, 2 * h + 1)),
        fixed(low.shape),
        pl.BlockSpec((VD + 16, rows), lambda h: (h, 0)),
        fixed(tables[0].shape),
        fixed(tables[1].shape),
    ]
    outs, out_specs, scratch = [], [], []
    for i, (want, spec, width) in enumerate(((want_q, col, VD), (want_k, pair, 2 * VD))):
        if want:
            if sums[i] is not None:
                ins.append(sums[i])
                in_specs.append(spec)
            outs.append(shape((rows, heads * width), BF16 if finish[i] else F32))
            out_specs.append(spec)
            scratch += [pltpu.VMEM((rows, VD), F32)] * (width // VD)
    kind = ("q" if want_q else "") + ("k" if want_k else "")
    return call(
        body,
        outs,
        ins,
        grid=(heads,),
        in_specs=in_specs,
        out_specs=out_specs,
        scratch=scratch,
        name=f"attend_back_{kind}{slot}",
    )


def middle_kernel(x, heads_out, mine, theirs, gain, spot):
    rows, wide = x.shape
    half = wide // 2
    count = len(heads_out)
    cols = heads_out[0].shape[1]
    tile = 256

    def body(spot_ref, x_ref, gain_ref, *refs):
        ho, wm, wt = refs[:count], refs[count : 2 * count], refs[2 * count : 3 * count]
        resid_ref, normed_ref, inv_ref = refs[3 * count :]
        total = jnp.zeros((tile, 1), F32)
        for side, weights in ((0, wm), (1, wt)):
            at = pl.ds(pl.multiple_of((spot_ref[1] ^ side) * half, 128), half)
            value = x_ref[:, at].astype(F32)
            for k in range(count):
                value = value + dot(ho[k][...], weights[k][...], 1, 1)
            resid_ref[:, at] = value
            total = total + jnp.sum(value * value, axis=1, keepdims=True)
        inv = lax.rsqrt(total / wide + EPSILON)
        inv_ref[...] = inv
        normed_ref[...] = (resid_ref[...] * inv * gain_ref[...]).astype(BF16)

    def tall(width):
        return pl.BlockSpec((tile, width), lambda i: (i, 0))

    return call(
        body,
        [shape((rows, wide), F32), shape((rows, wide), BF16), shape((rows, 1), F32)],
        [spot, x, gain] + heads_out + mine + theirs,
        grid=(rows // tile,),
        in_specs=[whole(pltpu.SMEM), tall(wide), fixed(gain.shape)]
        + [tall(cols)] * count
        + [fixed(mine[0].shape)] * (2 * count),
        out_specs=[tall(wide), tall(wide), tall(1)],
        name="middle",
    )


def ffn_kernel(x, dy, weights):
    rows, wide = x.shape
    cols = weights.shape[1] // 3
    tile = 256
    steps = cols // tile

    def body(x_ref, dy_ref, gate_w, up_w, down_w, hidden_ref, dgate_ref, dup_ref):
        gate = dot(x_ref[...], gate_w[...], 1, 0)
        up = dot(x_ref[...], up_w[...], 1, 0)
        grad = dot(dy_ref[...], down_w[...], 1, 0)
        sig = jax.nn.sigmoid(gate)
        active = gate * sig
        hidden_ref[...] = (active * up).astype(BF16)
        dgate_ref[...] = (grad * up * sig * (1.0 + gate * (1.0 - sig))).astype(BF16)
        dup_ref[...] = (grad * active).astype(BF16)

    def slab(part):
        return pl.BlockSpec((wide, tile), lambda i: (0, part * steps + i))

    strip = pl.BlockSpec((rows, tile), lambda i: (0, i))
    return call(
        body,
        [shape((rows, cols), BF16)] * 3,
        [x, dy, weights, weights, weights],
        grid=(steps,),
        in_specs=[fixed(x.shape), fixed(dy.shape), slab(0), slab(1), slab(2)],
        out_specs=[strip] * 3,
        name="ffn",
    )


def quarters_kernel(terms, spot, count, name, norm=None):
    rows = terms[0][0].shape[0]
    wide = terms[0][1].shape[0]
    cols = wide // count
    n = len(terms)

    def body(spot_ref, *refs):
        lefts, weights = refs[:n], refs[n : 2 * n]
        rest = refs[2 * n :]
        if norm is not None:
            x_ref, inv_ref, gain_ref = rest[:3]
            rest = rest[3:]
            col_ref, row_ref = rest[count:]
        outs = rest[:count]
        pos = pl.program_id(0)
        value = dot(lefts[0][...], weights[0][...], 1, 1)
        for i in range(1, n):
            value = value + dot(lefts[i][...], weights[i][...], 1, 1)
        if norm is not None:
            weighed = value * (x_ref[...].astype(F32) * inv_ref[...])
            col_ref[...] = jnp.sum(weighed, axis=0, keepdims=True)
            ones = jnp.ones((8, cols), BF16)
            row_sum = dot(ones, (weighed * gain_ref[...]).astype(BF16), 1, 1)

            @pl.when(pos == 0)
            def _():
                row_ref[...] = row_sum

            @pl.when(pos > 0)
            def _():
                row_ref[...] += row_sum

        value = value.astype(BF16)
        for k in range(count):

            @pl.when(spot_ref[0] ^ k == pos)
            def _(k=k):
                outs[k][0:rows, :] = value

        if norm is not None:

            @pl.when(pos == count - 1)
            def _():
                total = row_ref[0:1, :]
                high = total.astype(BF16).astype(F32)
                packed = []
                for part in (high, total - high):
                    packed += [part[:, at : at + cols] for at in range(0, rows, cols)]
                packed.append(jnp.zeros((16 - len(packed), cols), F32))
                packed = jnp.concatenate(packed, axis=0).astype(BF16)
                for out in outs:
                    out[rows : rows + 16, :] = packed

    ins = [spot] + [t[0] for t in terms] + [t[1] for t in terms]
    in_specs = [whole(pltpu.SMEM)] + [fixed(t[0].shape) for t in terms]
    for left, _, first in terms:
        width = left.shape[1]
        in_specs.append(pl.BlockSpec((cols, width), lambda i, at=first // width: (i, at)))
    tall = rows if norm is None else rows + 16
    outs = [shape((tall, cols), BF16)] * count
    out_specs = [fixed((tall, cols))] * count
    scratch = []
    if norm is not None:
        ins += list(norm)
        in_specs += [
            pl.BlockSpec((rows, cols), lambda i: (0, i)),
            fixed((rows, 1)),
            pl.BlockSpec((1, cols), lambda i: (0, i)),
        ]
        outs = outs + [shape((1, wide), F32)]
        out_specs = out_specs + [pl.BlockSpec((1, cols), lambda i: (0, i))]
        scratch = [pltpu.VMEM((8, rows), F32)]
    return call(
        body, outs, ins, grid=(count,), in_specs=in_specs, out_specs=out_specs, scratch=scratch, name=name
    )


def mid_back_kernel(dgate, dup, gate_w, gate_first, up_w, up_first, head_at, count):
    rows, cols = dgate.shape
    wide = gate_w.shape[0]
    tile = 384
    steps = wide // tile
    part = rows // count

    def body(at_ref, dgate_ref, dup_ref, g_ref, u_ref, *refs):
        outs = refs[:count]
        value = dot(dgate_ref[...], g_ref[...], 1, 1) + dot(dup_ref[...], u_ref[...], 1, 1)
        value = value.astype(BF16)
        for row in range(count):
            rows_of = value[row * part : (row + 1) * part, :]
            for k in range(count):

                @pl.when(at_ref[0] ^ k == row)
                def _(k=k, rows_of=rows_of):
                    outs[k][...] = rows_of

    return call(
        body,
        [shape((part, wide), BF16)] * count,
        [head_at, dgate, dup, gate_w, up_w],
        grid=(steps,),
        in_specs=[
            whole(pltpu.SMEM),
            fixed(dgate.shape),
            fixed(dup.shape),
            pl.BlockSpec((tile, cols), lambda i: (i, gate_first // cols)),
            pl.BlockSpec((tile, cols), lambda i: (i, up_first // cols)),
        ],
        out_specs=[pl.BlockSpec((part, tile), lambda i: (0, i))] * count,
        name="mid_back",
    )


def norm_mid_back_kernel(parts, resid, inv, gain, dy, spot):
    part, wide = parts[0].shape
    count = len(parts)

    def body(spot_ref, gain_ref, resid_ref, inv_ref, dy_ref, *refs):
        ins, (out_ref, col_ref) = refs[:count], refs[count:]
        grad = ins[0][...].astype(F32)
        for ref in ins[1:]:
            grad = grad + ref[...].astype(F32)
        inv_rows = inv_ref[...]
        unit = resid_ref[...] * inv_rows
        col_ref[...] = jnp.sum(grad * unit, axis=0, keepdims=True)
        e = grad * gain_ref[...]
        mean = jnp.sum(e * unit, axis=1, keepdims=True) / wide
        out_ref[...] = (dy_ref[...].astype(F32) + inv_rows * (e - unit * mean)).astype(BF16)

    def mine(width):
        return pl.BlockSpec((part, width), lambda i, spot_ref: (spot_ref[0], 0))

    def all_of(dims):
        return pl.BlockSpec(tuple(dims), lambda i, spot_ref: (0, 0))

    return pl.pallas_call(
        body,
        out_shape=[shape((part, wide), BF16), shape((1, wide), F32)],
        grid_spec=pltpu.PrefetchScalarGridSpec(
            num_scalar_prefetch=1,
            grid=(1,),
            in_specs=[all_of(gain.shape), mine(wide), mine(1), mine(wide)] + [all_of((part, wide))] * count,
            out_specs=[all_of((part, wide)), all_of((1, wide))],
        ),
        compiler_params=pltpu.CompilerParams(vmem_limit_bytes=VMEM_LIMIT),
        cost_estimate=work("norm_mid_back"),
        name="norm_mid_back",
    )(spot, gain, resid, inv, dy, *parts)


def head_back_kernel(branch, weight, first, cols, unit, two, fin, gain, lam):
    rows, wide = branch.shape
    heads = cols // VD

    def body(lam_ref, b_ref, weight_ref, unit_ref, two_ref, fin_ref, gain_ref, g_ref, sum_ref):
        grad = jnp.transpose(dot(b_ref[...], weight_ref[...], 1, 0))
        unit = unit_ref[...]
        out_two = two_ref[...]
        inv = fin_ref[2:3, :]
        f = grad * gain_ref[...] * KEEP
        mean = jnp.mean(f * unit, axis=0, keepdims=True)
        mixed_grad = inv * (f - unit * mean)
        g = mixed_grad.astype(BF16)
        g_ref[0:VD, :] = g
        g = g.astype(F32)
        delta_two = jnp.sum(g * out_two, axis=0, keepdims=True)
        mixed = unit / inv
        delta_one = jnp.sum(g * mixed, axis=0, keepdims=True) + lam_ref[0, 0] * delta_two
        stat = jnp.concatenate(
            [fin_ref[0:2, :], delta_one, delta_two, jnp.zeros((4, rows), F32)], axis=0
        )
        high = stat.astype(BF16).astype(F32)
        g_ref[VD : VD + 16, :] = jnp.concatenate([high, stat - high], axis=0).astype(BF16)
        gain_term = jnp.sum(grad * unit, axis=1, keepdims=True) * KEEP
        lam_term = -jnp.sum(mixed_grad * out_two, axis=1, keepdims=True)
        lanes = lax.broadcasted_iota(jnp.int32, (VD, 128), 1)
        sum_ref[...] = jnp.where(lanes == 0, gain_term, jnp.where(lanes == 1, lam_term, 0.0))

    row_spec = pl.BlockSpec((VD, rows), lambda h: (h, 0))
    stat_spec = pl.BlockSpec((8, rows), lambda h: (h, 0))
    slab = pl.BlockSpec((wide, VD), lambda h: (0, first // VD + h))
    return call(
        body,
        [shape((heads * (VD + 16), rows), BF16), shape((heads * VD, 128), F32)],
        [lam, branch, weight, unit, two, fin, gain],
        grid=(heads,),
        in_specs=[
            whole(pltpu.SMEM),
            fixed(branch.shape),
            slab,
            row_spec,
            row_spec,
            stat_spec,
            fixed(gain.shape),
        ],
        out_specs=[
            pl.BlockSpec((VD + 16, rows), lambda h: (h, 0)),
            pl.BlockSpec((VD, 128), lambda h: (h, 0)),
        ],
        name="head_back",
        flops=2 * rows * wide * cols,
    )


def outer_kernel(pairs, side, got, name, split=False):
    rows = pairs[0][0].shape[0]
    half = pairs[0][0].shape[1] // 2
    widths = [right.shape[1] for _, right in pairs]
    tile = 512 if all(w % 512 == 0 for w in widths) else 384
    steps = [w // tile for w in widths]
    starts = [sum(steps[:i]) for i in range(len(steps))]
    n = len(pairs)
    lefts = []
    for left, _ in pairs:
        if not any(left is other for other in lefts):
            lefts.append(left)
    left_of = [next(i for i, other in enumerate(lefts) if other is left) for left, _ in pairs]
    with_got = got is not None

    def body(side_ref, *refs):
        left_refs, right_refs = refs[: len(lefts)], refs[len(lefts) : len(lefts) + n]
        turned = refs[-1]
        out_refs = refs[-1 - n : -1] if split else [refs[-2]] * n
        got_ref = refs[len(lefts) + n]
        step = pl.program_id(0)
        for i in range(n):
            if i == 0 or left_of[i] != left_of[i - 1]:

                @pl.when(step == starts[i])
                def _(i=i):
                    turned[...] = jnp.transpose(left_refs[left_of[i]][...])

            @pl.when(jnp.logical_and(step >= starts[i], step < starts[i] + steps[i]))
            def _(i=i):
                value = dot(turned[...], right_refs[i][...], 1, 0)
                if with_got:
                    value = value + got_ref[...].astype(F32)
                out_refs[i][...] = value.astype(BF16)

    def right_spec(i):
        return pl.BlockSpec((rows, tile), lambda j, side_ref: (0, jnp.clip(j - starts[i], 0, steps[i] - 1)))

    def out_spec(i):
        return pl.BlockSpec((half, tile), lambda j, side_ref: (0, jnp.clip(j - starts[i], 0, steps[i] - 1)))

    strip = pl.BlockSpec((half, tile), lambda j, side_ref: (0, j))
    return pl.pallas_call(
        body,
        out_shape=[shape((half, w), BF16) for w in widths] if split else shape((half, sum(widths)), BF16),
        grid_spec=pltpu.PrefetchScalarGridSpec(
            num_scalar_prefetch=1,
            grid=(sum(steps),),
            in_specs=[pl.BlockSpec((rows, half), lambda j, side_ref: (0, side_ref[0]))] * len(lefts)
            + [right_spec(i) for i in range(n)]
            + ([strip] if with_got else []),
            out_specs=[out_spec(i) for i in range(n)] if split else strip,
            scratch_shapes=[pltpu.VMEM((half, rows), BF16)],
        ),
        compiler_params=pltpu.CompilerParams(vmem_limit_bytes=VMEM_LIMIT),
        cost_estimate=work(name),
        name=name,
    )(side, *lefts, *[right for _, right in pairs], *([got] if with_got else []))


def per_device(
    tokens,
    segment_ids,
    gain_attn,
    w_query,
    w_key,
    w_value,
    w_output,
    lambda_vec,
    gain_heads,
    gain_ffn,
    w_gate,
    w_up,
    w_down,
    grad_out,
):
    rows, slice_width = tokens.shape
    n_ctx = lax.axis_size("ctx")
    n_head = lax.axis_size("head")
    place = lax.axis_index("ctx")
    head = lax.axis_index("head")
    core = lax.axis_index("dp")
    group = segment_ids.shape[0]
    wide = slice_width * n_head
    cols = w_query.shape[1]
    heads = cols // VD
    spot = jnp.stack([head, core]).astype(jnp.int32)
    my_side = jnp.reshape(core, (1,)).astype(jnp.int32)
    other_side = 1 - my_side
    reach = n_ctx
    if n_ctx == 4 and group == 3072 and rows == 768:
        reach = n_ctx - 1

    kvqo_w = gather_rows(pack_kernel(w_key, w_value, w_query, w_output.T))
    downward = [[(i + slot, i) for i in range(n_ctx - slot)] for slot in range(reach)]
    x_units = head_gather(tokens)
    hidden_cols = w_gate.shape[1]
    gud_w = gather_rows(jnp.concatenate([w_gate, w_up, w_down.T], axis=1))

    lane = jnp.arange(128, dtype=jnp.int32)
    frequency = ROPE_BASE ** (-((lane % (HALF // 2)).astype(F32) * 2.0 / HALF))
    sign = jnp.where(lane % HALF < HALF // 2, -1.0, 1.0)[None, :]

    def starts_of(block):
        first_row = jnp.clip(block, 0, n_ctx - 1) * rows
        segs = lax.dynamic_slice_in_dim(segment_ids, first_row, rows, 0)
        return jnp.sum((segment_ids[None, :] < segs[:, None]).astype(jnp.int32), axis=1)

    def tables_of(block, before):
        row_index = jnp.clip(block, 0, n_ctx - 1) * rows + jnp.arange(rows, dtype=jnp.int32)
        angles = (row_index - before).astype(F32)[:, None] * frequency[None, :]
        return jnp.cos(angles), jnp.sin(angles) * sign

    def reach_of(block, before):
        before = jnp.where(block < n_ctx, before, jnp.int32(1 << 30))
        low = jnp.broadcast_to(before[None, :], (8, rows))
        return low, jnp.concatenate([jnp.reshape(block, (1,)), before[::ATTN_TILE]]).astype(jnp.int32)

    own_starts = starts_of(place)
    tables = [tables_of(place, own_starts)]
    for slot in range(1, reach):
        tables.append(tables_of(place - slot, starts_of(place - slot)))
    cosine, sine = tables[0]
    low, meta = reach_of(place, own_starts)
    token_slots = [tokens]
    for slot in range(1, reach):
        token_slots.append(lax.ppermute(token_slots[-1], "ctx", [(i, i + 1) for i in range(slot - 1, n_ctx - 1)]))
    exp_one = jnp.exp(jnp.sum(lambda_vec[0] * lambda_vec[1]))
    exp_two = jnp.exp(jnp.sum(lambda_vec[2] * lambda_vec[3]))
    lam = jnp.reshape(exp_one - exp_two + LAMBDA_START, (1, 1))

    gain_in = gain_attn[None, :]
    gain_mid = gain_ffn[None, :]

    x_units[0] = after(x_units[0], *[t for pair in tables for t in pair])
    normed_in, x_full, inv_in = norm_in_kernel(x_units, gain_in, spot, True)
    dy_units = head_gather(after(grad_out, normed_in))
    dy = place_cols_kernel(dy_units, spot)
    kvqo_w = after(kvqo_w, dy)
    kv, queries = project_kernel(normed_in, kvqo_w, 2 * cols, cols, cosine, sine)
    query_slots = [queries]
    half = wide // 2
    o_half = lax.dynamic_slice(kvqo_w, (core * half, 3 * cols), (half, cols))
    kv_slots = [kv]

    def keys_of(slot, units):
        normed = norm_in_kernel(units, gain_in, spot, False)[0]
        kv_slots.extend(project_kernel(normed, kvqo_w, 2 * cols, 0, *tables[slot]))

    def attend(slot, state):
        return attend_kernel(
            slot,
            slot == 0,
            slot == reach - 1,
            meta,
            lam,
            queries,
            kv_slots[slot],
            low,
            gain_heads[None, :],
            state,
        )

    state = None
    units = head_gather(after(token_slots[1], dy_units[1])) if reach > 1 else dy_units
    state = attend(0, state)
    for slot in range(1, reach):
        coming = units
        if slot + 1 < reach:
            units = head_gather(after(token_slots[slot + 1], state[0], *coming[1:]))
        keys_of(slot, [after(coming[0], state[0])] + coming[1:])
        if slot == reach - 1:
            o_units = head_gather(after(o_half, state[0], *coming[1:]))
        state = attend(slot, state)
    if reach == 1:
        o_units = head_gather(o_half)
    head_out, unit_head, out_two, finish = state
    ho_units = head_gather(head_out)
    o_theirs = [core_swap(after(u, head_out)) for u in o_units]
    resid, normed_mid, inv_mid = middle_kernel(x_full, ho_units, o_units, o_theirs, gain_mid, spot)
    hidden, dgate, dup = ffn_kernel(normed_mid, dy, gud_w)
    for slot in range(1, reach):
        sent = after(query_slots[-1], dgate)
        query_slots.append(lax.ppermute(sent, "ctx", [(i, i - 1) for i in range(1, n_ctx + 1 - slot)]))
    mid_parts = mid_back_kernel(dgate, dup, gud_w, 0, gud_w, hidden_cols, spot, n_head)
    mid_got = [head_move(mid_parts[k], k) for k in range(1, n_head)]

    d_theirs = outer_kernel([(dy, hidden)], after(other_side, mid_parts[0]), None, "d_grads_theirs")
    d_got = core_swap(d_theirs)
    y_parts = quarters_kernel([(hidden, gud_w, 2 * hidden_cols)], after(spot, d_theirs), n_head, "down")
    d_sums = outer_kernel([(dy, hidden)], after(my_side, y_parts[0]), d_got, "d_grads")
    d_total = scatter_rows(d_sums)
    gu_pairs = [(normed_mid, dgate), (normed_mid, dup)]
    gu_theirs = outer_kernel(gu_pairs, after(other_side, d_sums), None, "gu_grads_theirs")
    gu_got = core_swap(gu_theirs)
    mid_got[0] = after(mid_got[0], gu_theirs, *query_slots[1:])
    branch_rows, ffn_gain_term = norm_mid_back_kernel(
        [mid_parts[0]] + mid_got, resid, inv_mid, gain_mid, dy, spot
    )
    branch_units = head_gather(branch_rows)
    g_sums, u_sums = outer_kernel(gu_pairs, after(my_side, branch_rows), gu_got, "gu_grads", split=True)
    g_total = scatter_rows(g_sums)
    branch_units[0] = after(branch_units[0], d_total)
    branch = place_rows(
        branch_units, jnp.stack([head ^ k for k in range(n_head)]).astype(jnp.int32), n_head
    )

    grads, head_sums = head_back_kernel(
        branch, kvqo_w, 3 * cols, cols, unit_head, out_two, finish, gain_heads[:, None], lam
    )
    grad_slots = [grads]

    for slot in range(1, reach):
        grad_slots.append(lax.ppermute(grads, "ctx", downward[slot]))

    def back(slot, finish, on, sums, *gates):
        block_low, block_meta = low, meta
        if on:
            block_low, block_meta = reach_of(place + slot, starts_of(place + slot))
        return attend_back_kernel(
            slot,
            finish,
            after(block_meta, *gates),
            lam,
            query_slots[slot] if on else queries,
            kv if on else kv_slots[slot],
            block_low,
            grad_slots[slot] if on else grads,
            (cosine, sine),
            sums,
        )

    y_got = [head_move(after(y_parts[k], branch), k) for k in range(1, n_head)]
    only = reach == 1
    dq, dkv = back(0, (only, only), False, (None, None))
    last = dq
    for slot in reversed(range(1, reach)):
        arrived = [grad_slots[1]] + y_got if slot == 1 else []
        dq = back(slot, (slot == 1, False), False, (dq, False), last, *arrived)[0]
        last = dq
    dq_pre = dq

    my_cols = head * slice_width
    output = lax.dynamic_slice_in_dim(resid, my_cols, slice_width, 1) + after(y_parts[0], dq_pre).astype(F32)
    for got in y_got:
        output = output + got.astype(F32)
    output = output.astype(BF16)
    last = output
    for slot in range(1, reach):
        dkv = back(slot, (False, slot == reach - 1), True, (False, dkv), last)[0]
        last = dkv
        if slot == 1:
            u_sums = after(u_sums, dkv)
    u_total = scatter_rows(after(u_sums, g_total, *grad_slots))
    dkv_pre = dkv

    oqkv_pairs = [(branch, head_out), (normed_in, dq_pre), (normed_in, dkv_pre)]
    oqkv_theirs = outer_kernel(oqkv_pairs, other_side, None, "oqkv_grads_theirs")
    oqkv_got = core_swap(oqkv_theirs)
    in_parts = quarters_kernel(
        [(dq_pre, kvqo_w, 2 * cols), (dkv_pre, kvqo_w, 0)],
        after(spot, oqkv_theirs),
        n_head,
        "in_back",
        norm=(x_full, inv_in, gain_in),
    )
    oqkv_sums = outer_kernel(oqkv_pairs, after(my_side, in_parts[0]), oqkv_got, "oqkv_grads")
    oqkv_total = scatter_rows(after(oqkv_sums, u_total))
    oq_total, kv_total = oqkv_total[:, : 2 * cols], oqkv_total[:, 2 * cols :]
    head_sums = jnp.sum(head_sums.reshape(heads, VD, 128), axis=0)
    small = jnp.concatenate(
        [
            in_parts[n_head][0],
            ffn_gain_term[0],
            head_sums[:, 0],
            jnp.full((128,), jnp.sum(head_sums[:, 1]), F32),
        ]
    ).reshape(-1, 128)
    small = line_sum(small)
    in_got = [head_move(in_parts[k], k) for k in range(1, n_head)]
    grad_in = jnp.zeros((rows + 16, slice_width), F32)
    for got in [in_parts[0]] + in_got:
        grad_in = grad_in + got.astype(F32)
    count = rows // slice_width
    row_sums = (grad_in[rows : rows + count] + grad_in[rows + count : rows + 2 * count]).reshape(rows, 1)
    grad_in = grad_in[:rows]
    my_gain = lax.dynamic_slice_in_dim(gain_in, my_cols, slice_width, 1)
    my_branch = lax.dynamic_slice_in_dim(branch, my_cols, slice_width, 1).astype(F32)
    unit_in = tokens.astype(F32) * inv_in
    grad_tokens = my_branch + inv_in * (grad_in * my_gain - unit_in * (row_sums / wide))

    small = head_sum(after(small, *in_got)).reshape(-1)
    attn_gain_grad = small[:wide]
    ffn_gain_grad = small[wide : 2 * wide]
    heads_gain_grad = small[2 * wide : 2 * wide + VD]
    lambda_scalar = small[2 * wide + VD]
    grad_lambda = jnp.stack(
        [
            lambda_scalar * exp_one * lambda_vec[1],
            lambda_scalar * exp_one * lambda_vec[0],
            -lambda_scalar * exp_two * lambda_vec[3],
            -lambda_scalar * exp_two * lambda_vec[2],
        ],
        axis=0,
    )
    grad_kv = kv_total.astype(F32)
    grad_key = jnp.concatenate([grad_kv[:, 2 * h * VD : (2 * h + 1) * VD] for h in range(heads)], axis=1)
    grad_value = jnp.concatenate(
        [grad_kv[:, (2 * h + 1) * VD : (2 * h + 2) * VD] for h in range(heads)], axis=1
    )
    return (
        output,
        grad_tokens,
        attn_gain_grad,
        oq_total[:, cols:].astype(F32),
        grad_key,
        grad_value,
        oq_total[:, :cols].astype(F32).T,
        grad_lambda,
        heads_gain_grad,
        ffn_gain_grad,
        g_total.astype(F32),
        u_total.astype(F32),
        d_total.astype(F32).T,
    )


def solution(mesh):
    split = P(("dp", "ctx"), "head")
    turned = P("head", ("dp", "ctx"))
    in_specs = (
        split,
        P("dp"),
        P(),
        split,
        split,
        split,
        turned,
        P(),
        P(),
        P(),
        split,
        split,
        turned,
        split,
    )
    out_specs = (
        split,
        split,
        P(),
        split,
        split,
        split,
        turned,
        P(),
        P(),
        P(),
        split,
        split,
        turned,
    )
    return jax.shard_map(
        per_device, mesh=mesh, in_specs=in_specs, out_specs=out_specs, check_vma=False
    )
```

```python
import functools
import math

import jax
import jax.numpy as jnp
from jax import lax
from jax.experimental import pallas as pl
from jax.experimental.pallas import tpu as pltpu
from jax.sharding import PartitionSpec as P

HALF = 64
VD = 128
LAYER = 6
EPSILON = 1e-06
ROPE_BASE = 10000.0
MAX_START = -1e30
MASKED = -2e38
SCALE = HALF ** (-0.5)
LAMBDA_START = 0.8 - 0.6 * math.exp(-0.3 * (LAYER - 1))
KEEP = 1.0 - LAMBDA_START

BF16 = jnp.bfloat16
F32 = jnp.float32
VMEM_LIMIT = 60 * 1024 * 1024


LONG = {"place_rows": 1000, "norm_mid_back": 1000, "down": 1000}


def work(name):
    return pl.CostEstimate(flops=LONG.get(name, 0) * 10**9 + 1, bytes_accessed=1, transcendentals=0)


def shape(dims, dtype):
    return jax.ShapeDtypeStruct(tuple(dims), dtype)


def whole(memory=pltpu.VMEM):
    return pl.BlockSpec(memory_space=memory)


def fixed(dims):
    zeros = (0,) * len(dims)
    return pl.BlockSpec(tuple(dims), lambda *_: zeros)


def call(body, outs, ins, *, name, grid=None, in_specs=None, out_specs=None, scratch=(), flops=0, move=0):
    if in_specs is None:
        in_specs = [whole(pltpu.SMEM) if a.ndim == 1 and a.dtype == jnp.int32 else whole() for a in ins]
    if out_specs is None:
        out_specs = [whole() for _ in outs]
    kwargs = {}
    if grid is not None:
        kwargs["grid"] = grid
    if not move:
        move = sum(a.size * a.dtype.itemsize for a in list(ins) + list(outs))
    return pl.pallas_call(
        body,
        out_shape=list(outs),
        in_specs=in_specs,
        out_specs=out_specs,
        scratch_shapes=list(scratch),
        compiler_params=pltpu.CompilerParams(vmem_limit_bytes=VMEM_LIMIT),
        cost_estimate=work(name),
        name=name,
        **kwargs,
    )(*ins)


def dot(left, right, left_dim, right_dim):
    return lax.dot_general(
        left, right, (((left_dim,), (right_dim,)), ((), ())), preferred_element_type=F32
    )


def xor_pairs(count, step):
    return [(i, i ^ step) for i in range(count)]


def head_move(value, step):
    return lax.ppermute(value, "head", xor_pairs(lax.axis_size("head"), step))


def core_swap(value):
    return lax.ppermute(value, "dp", xor_pairs(lax.axis_size("dp"), 1))


def head_gather(unit):
    return [unit] + [head_move(unit, k) for k in range(1, lax.axis_size("head"))]


def after(value, *others):
    return lax.optimization_barrier((value,) + others)[0]


def place_rows(units, places, count):
    rows, cols = units[0].shape

    def body(at_ref, *refs):
        out = refs[-1]
        for i, ref in enumerate(refs[:-1]):
            start = pl.multiple_of(at_ref[i] * rows, 16)
            out[pl.ds(start, rows), :] = ref[...]

    return call(
        body, [shape((rows * count, cols), units[0].dtype)], [places] + list(units), name="place_rows"
    )[0]


def gather_rows(unit):
    return lax.all_gather(unit, ("dp", "ctx"), axis=0, tiled=True)


def scatter_rows(sums):
    return lax.psum_scatter(sums, "ctx", scatter_dimension=0, tiled=True)


def line_sum(value):
    value = value + core_swap(value)
    step = 1
    while step < lax.axis_size("ctx"):
        value = value + lax.ppermute(value, "ctx", xor_pairs(lax.axis_size("ctx"), step))
        step *= 2
    return value


def head_sum(value):
    step = 1
    while step < lax.axis_size("head"):
        value = value + head_move(value, step)
        step *= 2
    return value


def turn(value, cosine, sine, sign):
    groups = []
    lanes = lax.broadcasted_iota(jnp.int32, cosine.shape, 1)
    lower = lanes % HALF < HALF // 2
    for i in range(value.shape[1] // 128):
        part = value[:, i * 128 : (i + 1) * 128]
        swapped = jnp.where(
            lower, pltpu.roll(part, 128 - HALF // 2, axis=1), pltpu.roll(part, HALF // 2, axis=1)
        )
        groups.append(part * cosine + sign * (swapped * sine))
    return jnp.concatenate(groups, axis=1)


def half_lanes(value):
    lanes = lax.broadcasted_iota(jnp.int32, value.shape, 1)
    zero = jnp.zeros_like(value)
    return jnp.where(lanes < HALF, value, zero), jnp.where(lanes < HALF, zero, value)


def pack_kernel(keys, values, *others):
    rows, cols = keys.shape
    heads = cols // VD

    def body(k_ref, v_ref, *refs):
        out = refs[-1]
        for h in range(heads):
            at = 2 * h * VD
            out[:, at : at + VD] = k_ref[:, h * VD : (h + 1) * VD]
            out[:, at + VD : at + 2 * VD] = v_ref[:, h * VD : (h + 1) * VD]
        at = 2 * cols
        for ref in refs[:-1]:
            out[:, at : at + ref.shape[1]] = ref[...]
            at += ref.shape[1]

    width = 2 * cols + sum(other.shape[1] for other in others)
    return call(body, [shape((rows, width), keys.dtype)], [keys, values, *others], name="pack")[0]


def norm_in_kernel(units, gain, spot, keep):
    rows, cols = units[0].shape
    count = len(units)
    wide = cols * count
    tile = 256

    def body(spot_ref, gain_ref, *refs):
        ins, outs = refs[:count], refs[count:]
        total = jnp.zeros((tile, 1), F32)
        for ref in ins:
            v = ref[...].astype(F32)
            total = total + jnp.sum(v * v, axis=1, keepdims=True)
        inv = lax.rsqrt(total / wide + EPSILON)
        for k, ref in enumerate(ins):
            at = pl.ds(pl.multiple_of((spot_ref[0] ^ k) * cols, 128), cols)
            v = ref[...]
            outs[0][:, at] = (v.astype(F32) * inv * gain_ref[:, at]).astype(BF16)
            if keep:
                outs[1][:, at] = v
        if keep:
            outs[2][...] = inv

    def tall(w):
        return pl.BlockSpec((tile, w), lambda i: (i, 0))

    outs, out_specs = [shape((rows, wide), BF16)], [tall(wide)]
    if keep:
        outs += [shape((rows, wide), BF16), shape((rows, 1), F32)]
        out_specs += [tall(wide), tall(1)]
    return call(
        body,
        outs,
        [spot, gain] + units,
        grid=(rows // tile,),
        in_specs=[whole(pltpu.SMEM), fixed(gain.shape)] + [tall(cols)] * count,
        out_specs=out_specs,
        name="norm_in",
    )


def project_kernel(x, weight, width, more, cosine, sine):
    rows, wide = x.shape
    tile = 384

    def body(x_ref, weight_ref, cos_ref, sin_ref, *outs):
        y = dot(x_ref[...], weight_ref[...], 1, 0)
        for h in range(width // (2 * VD)):
            at = 2 * h * VD
            outs[0][:, at : at + VD] = turn(y[:, at : at + VD], cos_ref[...], sin_ref[...], 1.0).astype(BF16)
            outs[0][:, at + VD : at + 2 * VD] = y[:, at + VD : at + 2 * VD].astype(BF16)
        if more:
            outs[1][...] = turn(y[:, width:], cos_ref[...], sin_ref[...], 1.0).astype(BF16)

    def tall(w):
        return pl.BlockSpec((tile, w), lambda i: (i, 0))

    widths = [width] + ([more] if more else [])
    return call(
        body,
        [shape((rows, w), BF16) for w in widths],
        [x, weight, cosine, sine],
        grid=(rows // tile,),
        in_specs=[tall(wide), fixed((wide, width + more)), tall(128), tall(128)],
        out_specs=[tall(w) for w in widths],
        name="project",
    )


def place_cols_kernel(units, spot):
    rows, cols = units[0].shape
    count = len(units)

    def body(spot_ref, *refs):
        for k, ref in enumerate(refs[:count]):
            at = pl.ds(pl.multiple_of((spot_ref[0] ^ k) * cols, 128), cols)
            refs[count][:, at] = ref[...]

    return call(body, [shape((rows, cols * count), BF16)], [spot] + units, name="place_cols")[0]


ATTN_TILE = 384


def spans(meta_ref, slot, qi, rows):
    base = (meta_ref[0] - slot) * rows
    first = meta_ref[1 + qi]
    end = (qi + 1) * ATTN_TILE if slot == 0 else rows
    later = end - ATTN_TILE
    present = meta_ref[0] >= slot
    if later == 0:
        return [(slice(0, end), jnp.logical_and(present, first < base + end))]
    return [
        (slice(0, end), jnp.logical_and(present, first < base + later)),
        (
            slice(later, end),
            jnp.logical_and(present, jnp.logical_and(first >= base + later, first < base + end)),
        ),
    ]


def score_mask(meta_ref, slot, qi, at, rows, first):
    dims = (at.stop - at.start, ATTN_TILE)
    key_at = lax.broadcasted_iota(jnp.int32, dims, 0) + ((meta_ref[0] - slot) * rows + at.start)
    ok = key_at >= first
    if slot == 0:
        query_at = lax.broadcasted_iota(jnp.int32, dims, 1) + (meta_ref[0] * rows + qi * ATTN_TILE)
        ok = jnp.logical_and(ok, key_at <= query_at)
    return ok


def attend_kernel(slot, first, last, meta, lam, q, kv, low, gain, state):
    rows = q.shape[0]
    heads = q.shape[1] // VD
    tile = ATTN_TILE
    tiles = rows // tile

    def body(meta_ref, lam_ref, q_ref, k_ref, v_ref, low_ref, gain_ref, *refs):
        if first:
            outs = refs
        else:
            acc_in, stat_in = refs[:2]
            outs = refs[2:]
        if last:
            head_ref, unit_ref, two_ref, fin_ref, acc, stat = outs
        else:
            acc, stat = outs
        if first:
            acc[...] = jnp.zeros_like(acc)
            stat[0:2, :] = jnp.full((2, rows), MAX_START, F32)
            stat[2:8, :] = jnp.zeros((6, rows), F32)
        else:
            acc[...] = acc_in[...]
            stat[...] = stat_in[...]
        for qi in range(tiles):
            cols = slice(qi * tile, (qi + 1) * tile)
            halves = half_lanes(q_ref[cols, :] * BF16(SCALE))
            for at, needed in spans(meta_ref, slot, qi, rows):

                @pl.when(needed)
                def _(qi=qi, at=at, cols=cols, halves=halves):
                    keys = k_ref[at, :]
                    vals = v_ref[at, :]
                    ok = score_mask(meta_ref, slot, qi, at, rows, low_ref[0:1, cols])
                    for half in range(2):
                        score = jnp.where(ok, dot(keys, halves[half], 1, 1), MASKED)
                        old = stat[half : half + 1, cols]
                        new = jnp.maximum(old, jnp.max(score, axis=0, keepdims=True))
                        prob = jnp.exp(score - new)
                        fade = jnp.exp(old - new)
                        stat[half : half + 1, cols] = new
                        stat[2 + half : 3 + half, cols] = stat[2 + half : 3 + half, cols] * fade + jnp.sum(
                            prob, axis=0, keepdims=True
                        )
                        to = slice(half * VD, (half + 1) * VD)
                        acc[to, cols] = acc[to, cols] * fade + dot(vals, prob.astype(BF16), 0, 0)

        if last:
            out_one = acc[0:VD, :] / stat[2:3, :]
            out_two = acc[VD : 2 * VD, :] / stat[3:4, :]
            mixed = out_one - lam_ref[0, 0] * out_two
            inv = lax.rsqrt(jnp.mean(mixed * mixed, axis=0, keepdims=True) + EPSILON)
            unit = mixed * inv
            unit_ref[...] = unit
            two_ref[...] = out_two
            fin_ref[0:2, :] = stat[0:2, :] + jnp.log(stat[2:4, :])
            fin_ref[2:3, :] = inv
            fin_ref[3:8, :] = jnp.zeros((5, rows), F32)
            head_ref[...] = (jnp.transpose(unit) * gain_ref[...] * KEEP).astype(BF16)

    col = pl.BlockSpec((rows, VD), lambda h: (0, h))
    acc_spec = pl.BlockSpec((2 * VD, rows), lambda h: (h, 0))
    stat_spec = pl.BlockSpec((8, rows), lambda h: (h, 0))
    row_spec = pl.BlockSpec((VD, rows), lambda h: (h, 0))
    key_spec = pl.BlockSpec((rows, VD), lambda h: (0, 2 * h))
    value_spec = pl.BlockSpec((rows, VD), lambda h: (0, 2 * h + 1))
    in_specs = [whole(pltpu.SMEM), whole(pltpu.SMEM), col, key_spec, value_spec, fixed(low.shape), fixed(gain.shape)]
    ins = [meta, lam, q, kv, kv, low, gain]
    if not first:
        in_specs += [acc_spec, stat_spec]
        ins += list(state)
    outs, out_specs, scratch = [], [], []
    if last:
        outs = [
            shape((rows, heads * VD), BF16),
            shape((heads * VD, rows), F32),
            shape((heads * VD, rows), F32),
            shape((heads * 8, rows), F32),
        ]
        out_specs = [col, row_spec, row_spec, stat_spec]
        scratch = [pltpu.VMEM((2 * VD, rows), F32), pltpu.VMEM((8, rows), F32)]
    else:
        outs = [shape((heads * 2 * VD, rows), F32), shape((heads * 8, rows), F32)]
        out_specs = [acc_spec, stat_spec]
    return call(
        body,
        outs,
        ins,
        grid=(heads,),
        in_specs=in_specs,
        out_specs=out_specs,
        scratch=scratch,
        name=f"attend_{slot}",
        flops=2 * heads * rows * rows * (2 * HALF + 2 * VD),
    )


def attend_back_kernel(slot, finish, meta, lam, q, kv, low, grad, tables, sums):
    rows = q.shape[0]
    heads = q.shape[1] // VD
    want_q, want_k = sums[0] is not False, sums[1] is not False

    def body(meta_ref, lam_ref, q_ref, k_ref, v_ref, low_ref, grad_ref, cos_ref, sin_ref, *refs):
        refs = list(refs)
        dq_in = refs.pop(0) if want_q and sums[0] is not None else None
        dkv_in = refs.pop(0) if want_k and sums[1] is not None else None
        dq_out = refs.pop(0) if want_q else None
        dkv_out = refs.pop(0) if want_k else None
        dq_acc = refs.pop(0) if want_q else None
        if want_k:
            dk_acc, dv_acc = refs
        if want_q:
            dq_acc[...] = jnp.zeros_like(dq_acc) if dq_in is None else dq_in[...]
        if want_k:
            dk_acc[...] = jnp.zeros_like(dk_acc) if dkv_in is None else dkv_in[:, :VD]
            dv_acc[...] = jnp.zeros_like(dv_acc) if dkv_in is None else dkv_in[:, VD:]
        lam_value = lam_ref[0, 0]
        parts = grad_ref[VD : VD + 16, :].astype(F32)
        stat = parts[0:8, :] + parts[8:16, :]
        for qi in range(rows // ATTN_TILE):
            cols = slice(qi * ATTN_TILE, (qi + 1) * ATTN_TILE)
            q_one, q_two = half_lanes(q_ref[cols, :] * BF16(SCALE))
            for at, needed in spans(meta_ref, slot, qi, rows):

                @pl.when(needed)
                def _(qi=qi, at=at, cols=cols, q_one=q_one, q_two=q_two):
                    keys = k_ref[at, :]
                    grads = grad_ref[0:VD, cols]
                    ok = score_mask(meta_ref, slot, qi, at, rows, low_ref[0:1, cols])
                    inner = dot(v_ref[at, :], grads, 1, 0)
                    one = jnp.exp(jnp.where(ok, dot(keys, q_one, 1, 1), MASKED) - stat[0:1, cols])
                    two = lam_value * jnp.exp(
                        jnp.where(ok, dot(keys, q_two, 1, 1), MASKED) - stat[1:2, cols]
                    )
                    d_one = (one * (inner - stat[2:3, cols])).astype(BF16)
                    d_two = (two * (stat[3:4, cols] - inner)).astype(BF16)
                    if want_q:
                        k_one, k_two = half_lanes(keys * BF16(SCALE))
                        dq_acc[cols, :] += dot(d_one, k_one, 0, 0) + dot(d_two, k_two, 0, 0)
                    if want_k:
                        dv_acc[at, :] += dot((one - two).astype(BF16), grads, 1, 1)
                        dk_acc[at, :] += dot(d_one, q_one, 1, 0) + dot(d_two, q_two, 1, 0)

        if want_q:
            if finish[0]:
                dq_out[...] = turn(dq_acc[...], cos_ref[...], sin_ref[...], -1.0).astype(BF16)
            else:
                dq_out[...] = dq_acc[...]
        if want_k:
            if finish[1]:
                dkv_out[:, :VD] = turn(dk_acc[...], cos_ref[...], sin_ref[...], -1.0).astype(BF16)
                dkv_out[:, VD:] = dv_acc[...].astype(BF16)
            else:
                dkv_out[:, :VD] = dk_acc[...]
                dkv_out[:, VD:] = dv_acc[...]

    col = pl.BlockSpec((rows, VD), lambda h: (0, h))
    pair = pl.BlockSpec((rows, 2 * VD), lambda h: (0, h))
    ins = [meta, lam, q, kv, kv, low, grad, tables[0], tables[1]]
    in_specs = [
        whole(pltpu.SMEM),
        whole(pltpu.SMEM),
        col,
        pl.BlockSpec((rows, VD), lambda h: (0, 2 * h)),
        pl.BlockSpec((rows, VD), lambda h: (0, 2 * h + 1)),
        fixed(low.shape),
        pl.BlockSpec((VD + 16, rows), lambda h: (h, 0)),
        fixed(tables[0].shape),
        fixed(tables[1].shape),
    ]
    outs, out_specs, scratch = [], [], []
    for i, (want, spec, width) in enumerate(((want_q, col, VD), (want_k, pair, 2 * VD))):
        if want:
            if sums[i] is not None:
                ins.append(sums[i])
                in_specs.append(spec)
            outs.append(shape((rows, heads * width), BF16 if finish[i] else F32))
            out_specs.append(spec)
            scratch += [pltpu.VMEM((rows, VD), F32)] * (width // VD)
    kind = ("q" if want_q else "") + ("k" if want_k else "")
    return call(
        body,
        outs,
        ins,
        grid=(heads,),
        in_specs=in_specs,
        out_specs=out_specs,
        scratch=scratch,
        name=f"attend_back_{kind}{slot}",
    )


def middle_kernel(x, heads_out, mine, theirs, gain, spot):
    rows, wide = x.shape
    half = wide // 2
    count = len(heads_out)
    cols = heads_out[0].shape[1]
    tile = 384

    def body(spot_ref, x_ref, gain_ref, *refs):
        ho, wm, wt = refs[:count], refs[count : 2 * count], refs[2 * count : 3 * count]
        resid_ref, normed_ref, inv_ref = refs[3 * count :]
        total = jnp.zeros((tile, 1), F32)
        for side, weights in ((0, wm), (1, wt)):
            at = pl.ds(pl.multiple_of((spot_ref[1] ^ side) * half, 128), half)
            value = x_ref[:, at].astype(F32)
            for k in range(count):
                value = value + dot(ho[k][...], weights[k][...], 1, 1)
            resid_ref[:, at] = value
            total = total + jnp.sum(value * value, axis=1, keepdims=True)
        inv = lax.rsqrt(total / wide + EPSILON)
        inv_ref[...] = inv
        normed_ref[...] = (resid_ref[...] * inv * gain_ref[...]).astype(BF16)

    def tall(width):
        return pl.BlockSpec((tile, width), lambda i: (i, 0))

    return call(
        body,
        [shape((rows, wide), F32), shape((rows, wide), BF16), shape((rows, 1), F32)],
        [spot, x, gain] + heads_out + mine + theirs,
        grid=(rows // tile,),
        in_specs=[whole(pltpu.SMEM), tall(wide), fixed(gain.shape)]
        + [tall(cols)] * count
        + [fixed(mine[0].shape)] * (2 * count),
        out_specs=[tall(wide), tall(wide), tall(1)],
        name="middle",
    )


def ffn_kernel(x, dy, weights):
    rows, wide = x.shape
    cols = weights.shape[1] // 3
    tile = 256
    steps = cols // tile

    def body(x_ref, dy_ref, gate_w, up_w, down_w, hidden_ref, dgate_ref, dup_ref):
        gate = dot(x_ref[...], gate_w[...], 1, 0)
        up = dot(x_ref[...], up_w[...], 1, 0)
        grad = dot(dy_ref[...], down_w[...], 1, 0)
        sig = jax.nn.sigmoid(gate)
        active = gate * sig
        hidden_ref[...] = (active * up).astype(BF16)
        dgate_ref[...] = (grad * up * sig * (1.0 + gate * (1.0 - sig))).astype(BF16)
        dup_ref[...] = (grad * active).astype(BF16)

    def slab(part):
        return pl.BlockSpec((wide, tile), lambda i: (0, part * steps + i))

    strip = pl.BlockSpec((rows, tile), lambda i: (0, i))
    return call(
        body,
        [shape((rows, cols), BF16)] * 3,
        [x, dy, weights, weights, weights],
        grid=(steps,),
        in_specs=[fixed(x.shape), fixed(dy.shape), slab(0), slab(1), slab(2)],
        out_specs=[strip] * 3,
        name="ffn",
    )


def quarters_kernel(terms, spot, count, name, norm=None):
    rows = terms[0][0].shape[0]
    wide = terms[0][1].shape[0]
    cols = wide // count
    n = len(terms)

    def body(spot_ref, *refs):
        lefts, weights = refs[:n], refs[n : 2 * n]
        rest = refs[2 * n :]
        if norm is not None:
            x_ref, inv_ref, gain_ref = rest[:3]
            rest = rest[3:]
            col_ref, row_ref = rest[count:]
        outs = rest[:count]
        pos = pl.program_id(0)
        value = dot(lefts[0][...], weights[0][...], 1, 1)
        for i in range(1, n):
            value = value + dot(lefts[i][...], weights[i][...], 1, 1)
        if norm is not None:
            weighed = value * (x_ref[...].astype(F32) * inv_ref[...])
            col_ref[...] = jnp.sum(weighed, axis=0, keepdims=True)
            ones = jnp.ones((8, cols), BF16)
            row_sum = dot(ones, (weighed * gain_ref[...]).astype(BF16), 1, 1)

            @pl.when(pos == 0)
            def _():
                row_ref[...] = row_sum

            @pl.when(pos > 0)
            def _():
                row_ref[...] += row_sum

        value = value.astype(BF16)
        for k in range(count):

            @pl.when(spot_ref[0] ^ k == pos)
            def _(k=k):
                outs[k][0:rows, :] = value

        if norm is not None:

            @pl.when(pos == count - 1)
            def _():
                total = row_ref[0:1, :]
                high = total.astype(BF16).astype(F32)
                packed = []
                for part in (high, total - high):
                    packed += [part[:, at : at + cols] for at in range(0, rows, cols)]
                packed.append(jnp.zeros((16 - len(packed), cols), F32))
                packed = jnp.concatenate(packed, axis=0).astype(BF16)
                for out in outs:
                    out[rows : rows + 16, :] = packed

    ins = [spot] + [t[0] for t in terms] + [t[1] for t in terms]
    in_specs = [whole(pltpu.SMEM)] + [fixed(t[0].shape) for t in terms]
    for left, _, first in terms:
        width = left.shape[1]
        in_specs.append(pl.BlockSpec((cols, width), lambda i, at=first // width: (i, at)))
    tall = rows if norm is None else rows + 16
    outs = [shape((tall, cols), BF16)] * count
    out_specs = [fixed((tall, cols))] * count
    scratch = []
    if norm is not None:
        ins += list(norm)
        in_specs += [
            pl.BlockSpec((rows, cols), lambda i: (0, i)),
            fixed((rows, 1)),
            pl.BlockSpec((1, cols), lambda i: (0, i)),
        ]
        outs = outs + [shape((1, wide), F32)]
        out_specs = out_specs + [pl.BlockSpec((1, cols), lambda i: (0, i))]
        scratch = [pltpu.VMEM((8, rows), F32)]
    return call(
        body, outs, ins, grid=(count,), in_specs=in_specs, out_specs=out_specs, scratch=scratch, name=name
    )


def mid_back_kernel(dgate, dup, gate_w, gate_first, up_w, up_first, head_at, count):
    rows, cols = dgate.shape
    wide = gate_w.shape[0]
    tile = 384
    steps = wide // tile
    part = rows // count

    def body(at_ref, dgate_ref, dup_ref, g_ref, u_ref, *refs):
        outs = refs[:count]
        value = dot(dgate_ref[...], g_ref[...], 1, 1) + dot(dup_ref[...], u_ref[...], 1, 1)
        value = value.astype(BF16)
        for row in range(count):
            rows_of = value[row * part : (row + 1) * part, :]
            for k in range(count):

                @pl.when(at_ref[0] ^ k == row)
                def _(k=k, rows_of=rows_of):
                    outs[k][...] = rows_of

    return call(
        body,
        [shape((part, wide), BF16)] * count,
        [head_at, dgate, dup, gate_w, up_w],
        grid=(steps,),
        in_specs=[
            whole(pltpu.SMEM),
            fixed(dgate.shape),
            fixed(dup.shape),
            pl.BlockSpec((tile, cols), lambda i: (i, gate_first // cols)),
            pl.BlockSpec((tile, cols), lambda i: (i, up_first // cols)),
        ],
        out_specs=[pl.BlockSpec((part, tile), lambda i: (0, i))] * count,
        name="mid_back",
    )


def norm_mid_back_kernel(parts, resid, inv, gain, dy, spot):
    part, wide = parts[0].shape
    count = len(parts)

    def body(spot_ref, gain_ref, resid_ref, inv_ref, dy_ref, *refs):
        ins, (out_ref, col_ref) = refs[:count], refs[count:]
        grad = ins[0][...].astype(F32)
        for ref in ins[1:]:
            grad = grad + ref[...].astype(F32)
        inv_rows = inv_ref[...]
        unit = resid_ref[...] * inv_rows
        col_ref[...] = jnp.sum(grad * unit, axis=0, keepdims=True)
        e = grad * gain_ref[...]
        mean = jnp.sum(e * unit, axis=1, keepdims=True) / wide
        out_ref[...] = (dy_ref[...].astype(F32) + inv_rows * (e - unit * mean)).astype(BF16)

    def mine(width):
        return pl.BlockSpec((part, width), lambda i, spot_ref: (spot_ref[0], 0))

    def all_of(dims):
        return pl.BlockSpec(tuple(dims), lambda i, spot_ref: (0, 0))

    return pl.pallas_call(
        body,
        out_shape=[shape((part, wide), BF16), shape((1, wide), F32)],
        grid_spec=pltpu.PrefetchScalarGridSpec(
            num_scalar_prefetch=1,
            grid=(1,),
            in_specs=[all_of(gain.shape), mine(wide), mine(1), mine(wide)] + [all_of((part, wide))] * count,
            out_specs=[all_of((part, wide)), all_of((1, wide))],
        ),
        compiler_params=pltpu.CompilerParams(vmem_limit_bytes=VMEM_LIMIT),
        cost_estimate=work("norm_mid_back"),
        name="norm_mid_back",
    )(spot, gain, resid, inv, dy, *parts)


def head_back_kernel(branch, weight, first, cols, unit, two, fin, gain, lam):
    rows, wide = branch.shape
    heads = cols // VD

    def body(lam_ref, b_ref, weight_ref, unit_ref, two_ref, fin_ref, gain_ref, g_ref, sum_ref):
        grad = jnp.transpose(dot(b_ref[...], weight_ref[...], 1, 0))
        unit = unit_ref[...]
        out_two = two_ref[...]
        inv = fin_ref[2:3, :]
        f = grad * gain_ref[...] * KEEP
        mean = jnp.mean(f * unit, axis=0, keepdims=True)
        mixed_grad = inv * (f - unit * mean)
        g = mixed_grad.astype(BF16)
        g_ref[0:VD, :] = g
        g = g.astype(F32)
        delta_two = jnp.sum(g * out_two, axis=0, keepdims=True)
        mixed = unit / inv
        delta_one = jnp.sum(g * mixed, axis=0, keepdims=True) + lam_ref[0, 0] * delta_two
        stat = jnp.concatenate(
            [fin_ref[0:2, :], delta_one, delta_two, jnp.zeros((4, rows), F32)], axis=0
        )
        high = stat.astype(BF16).astype(F32)
        g_ref[VD : VD + 16, :] = jnp.concatenate([high, stat - high], axis=0).astype(BF16)
        gain_term = jnp.sum(grad * unit, axis=1, keepdims=True) * KEEP
        lam_term = -jnp.sum(mixed_grad * out_two, axis=1, keepdims=True)
        lanes = lax.broadcasted_iota(jnp.int32, (VD, 128), 1)
        sum_ref[...] = jnp.where(lanes == 0, gain_term, jnp.where(lanes == 1, lam_term, 0.0))

    row_spec = pl.BlockSpec((VD, rows), lambda h: (h, 0))
    stat_spec = pl.BlockSpec((8, rows), lambda h: (h, 0))
    slab = pl.BlockSpec((wide, VD), lambda h: (0, first // VD + h))
    return call(
        body,
        [shape((heads * (VD + 16), rows), BF16), shape((heads * VD, 128), F32)],
        [lam, branch, weight, unit, two, fin, gain],
        grid=(heads,),
        in_specs=[
            whole(pltpu.SMEM),
            fixed(branch.shape),
            slab,
            row_spec,
            row_spec,
            stat_spec,
            fixed(gain.shape),
        ],
        out_specs=[
            pl.BlockSpec((VD + 16, rows), lambda h: (h, 0)),
            pl.BlockSpec((VD, 128), lambda h: (h, 0)),
        ],
        name="head_back",
        flops=2 * rows * wide * cols,
    )


def outer_kernel(pairs, side, got, name, split=False):
    rows = pairs[0][0].shape[0]
    half = pairs[0][0].shape[1] // 2
    widths = [right.shape[1] for _, right in pairs]
    tile = 512 if all(w % 512 == 0 for w in widths) else 384
    steps = [w // tile for w in widths]
    starts = [sum(steps[:i]) for i in range(len(steps))]
    n = len(pairs)
    lefts = []
    for left, _ in pairs:
        if not any(left is other for other in lefts):
            lefts.append(left)
    left_of = [next(i for i, other in enumerate(lefts) if other is left) for left, _ in pairs]
    with_got = got is not None

    def body(side_ref, *refs):
        left_refs, right_refs = refs[: len(lefts)], refs[len(lefts) : len(lefts) + n]
        turned = refs[-1]
        out_refs = refs[-1 - n : -1] if split else [refs[-2]] * n
        got_ref = refs[len(lefts) + n]
        step = pl.program_id(0)
        for i in range(n):
            if i == 0 or left_of[i] != left_of[i - 1]:

                @pl.when(step == starts[i])
                def _(i=i):
                    turned[...] = jnp.transpose(left_refs[left_of[i]][...])

            @pl.when(jnp.logical_and(step >= starts[i], step < starts[i] + steps[i]))
            def _(i=i):
                value = dot(turned[...], right_refs[i][...], 1, 0)
                if with_got:
                    value = value + got_ref[...].astype(F32)
                out_refs[i][...] = value.astype(BF16)

    def right_spec(i):
        return pl.BlockSpec((rows, tile), lambda j, side_ref: (0, jnp.clip(j - starts[i], 0, steps[i] - 1)))

    def out_spec(i):
        return pl.BlockSpec((half, tile), lambda j, side_ref: (0, jnp.clip(j - starts[i], 0, steps[i] - 1)))

    strip = pl.BlockSpec((half, tile), lambda j, side_ref: (0, j))
    return pl.pallas_call(
        body,
        out_shape=[shape((half, w), BF16) for w in widths] if split else shape((half, sum(widths)), BF16),
        grid_spec=pltpu.PrefetchScalarGridSpec(
            num_scalar_prefetch=1,
            grid=(sum(steps),),
            in_specs=[pl.BlockSpec((rows, half), lambda j, side_ref: (0, side_ref[0]))] * len(lefts)
            + [right_spec(i) for i in range(n)]
            + ([strip] if with_got else []),
            out_specs=[out_spec(i) for i in range(n)] if split else strip,
            scratch_shapes=[pltpu.VMEM((half, rows), BF16)],
        ),
        compiler_params=pltpu.CompilerParams(vmem_limit_bytes=VMEM_LIMIT),
        cost_estimate=work(name),
        name=name,
    )(side, *lefts, *[right for _, right in pairs], *([got] if with_got else []))


def per_device(
    tokens,
    segment_ids,
    gain_attn,
    w_query,
    w_key,
    w_value,
    w_output,
    lambda_vec,
    gain_heads,
    gain_ffn,
    w_gate,
    w_up,
    w_down,
    grad_out,
):
    rows, slice_width = tokens.shape
    n_ctx = lax.axis_size("ctx")
    n_head = lax.axis_size("head")
    place = lax.axis_index("ctx")
    head = lax.axis_index("head")
    core = lax.axis_index("dp")
    group = segment_ids.shape[0]
    wide = slice_width * n_head
    cols = w_query.shape[1]
    heads = cols // VD
    spot = jnp.stack([head, core]).astype(jnp.int32)
    my_side = jnp.reshape(core, (1,)).astype(jnp.int32)
    other_side = 1 - my_side
    reach = n_ctx
    if n_ctx == 4 and group == 3072 and rows == 768:
        reach = n_ctx - 1

    kvqo_w = gather_rows(pack_kernel(w_key, w_value, w_query, w_output.T))
    downward = [[(i + slot, i) for i in range(n_ctx - slot)] for slot in range(reach)]
    x_units = head_gather(tokens)
    hidden_cols = w_gate.shape[1]
    gud_w = gather_rows(jnp.concatenate([w_gate, w_up, w_down.T], axis=1))

    lane = jnp.arange(128, dtype=jnp.int32)
    frequency = ROPE_BASE ** (-((lane % (HALF // 2)).astype(F32) * 2.0 / HALF))
    sign = jnp.where(lane % HALF < HALF // 2, -1.0, 1.0)[None, :]

    def starts_of(block):
        first_row = jnp.clip(block, 0, n_ctx - 1) * rows
        segs = lax.dynamic_slice_in_dim(segment_ids, first_row, rows, 0)
        return jnp.sum((segment_ids[None, :] < segs[:, None]).astype(jnp.int32), axis=1)

    def tables_of(block, before):
        row_index = jnp.clip(block, 0, n_ctx - 1) * rows + jnp.arange(rows, dtype=jnp.int32)
        angles = (row_index - before).astype(F32)[:, None] * frequency[None, :]
        return jnp.cos(angles), jnp.sin(angles) * sign

    def reach_of(block, before):
        before = jnp.where(block < n_ctx, before, jnp.int32(1 << 30))
        low = jnp.broadcast_to(before[None, :], (8, rows))
        return low, jnp.concatenate([jnp.reshape(block, (1,)), before[::ATTN_TILE]]).astype(jnp.int32)

    own_starts = starts_of(place)
    tables = [tables_of(place, own_starts)]
    for slot in range(1, reach):
        tables.append(tables_of(place - slot, starts_of(place - slot)))
    cosine, sine = tables[0]
    low, meta = reach_of(place, own_starts)
    token_slots = [tokens]
    for slot in range(1, reach):
        token_slots.append(lax.ppermute(token_slots[-1], "ctx", [(i, i + 1) for i in range(slot - 1, n_ctx - 1)]))
    exp_one = jnp.exp(jnp.sum(lambda_vec[0] * lambda_vec[1]))
    exp_two = jnp.exp(jnp.sum(lambda_vec[2] * lambda_vec[3]))
    lam = jnp.reshape(exp_one - exp_two + LAMBDA_START, (1, 1))

    gain_in = gain_attn[None, :]
    gain_mid = gain_ffn[None, :]

    x_units[0] = after(x_units[0], *[t for pair in tables for t in pair])
    normed_in, x_full, inv_in = norm_in_kernel(x_units, gain_in, spot, True)
    dy_units = head_gather(after(grad_out, normed_in))
    dy = place_cols_kernel(dy_units, spot)
    kvqo_w = after(kvqo_w, dy)
    kv, queries = project_kernel(normed_in, kvqo_w, 2 * cols, cols, cosine, sine)
    query_slots = [queries]
    half = wide // 2
    o_half = lax.dynamic_slice(kvqo_w, (core * half, 3 * cols), (half, cols))
    kv_slots = [kv]

    def keys_of(slot, units):
        normed = norm_in_kernel(units, gain_in, spot, False)[0]
        kv_slots.extend(project_kernel(normed, kvqo_w, 2 * cols, 0, *tables[slot]))

    def attend(slot, state):
        return attend_kernel(
            slot,
            slot == 0,
            slot == reach - 1,
            meta,
            lam,
            queries,
            kv_slots[slot],
            low,
            gain_heads[None, :],
            state,
        )

    state = None
    units = head_gather(after(token_slots[1], dy_units[1])) if reach > 1 else dy_units
    state = attend(0, state)
    for slot in range(1, reach):
        coming = units
        if slot + 1 < reach:
            units = head_gather(after(token_slots[slot + 1], state[0], *coming[1:]))
        keys_of(slot, [after(coming[0], state[0])] + coming[1:])
        if slot == reach - 1:
            o_units = head_gather(after(o_half, state[0], *coming[1:]))
        state = attend(slot, state)
    if reach == 1:
        o_units = head_gather(o_half)
    head_out, unit_head, out_two, finish = state
    ho_units = head_gather(head_out)
    o_theirs = [core_swap(after(u, head_out)) for u in o_units]
    resid, normed_mid, inv_mid = middle_kernel(x_full, ho_units, o_units, o_theirs, gain_mid, spot)
    hidden, dgate, dup = ffn_kernel(normed_mid, dy, gud_w)
    for slot in range(1, reach):
        sent = after(query_slots[-1], dgate)
        query_slots.append(lax.ppermute(sent, "ctx", [(i, i - 1) for i in range(1, n_ctx + 1 - slot)]))
    mid_parts = mid_back_kernel(dgate, dup, gud_w, 0, gud_w, hidden_cols, spot, n_head)
    mid_got = [head_move(mid_parts[k], k) for k in range(1, n_head)]

    d_theirs = outer_kernel([(dy, hidden)], after(other_side, mid_parts[0]), None, "d_grads_theirs")
    d_got = core_swap(d_theirs)
    y_parts = quarters_kernel([(hidden, gud_w, 2 * hidden_cols)], after(spot, d_theirs), n_head, "down")
    d_sums = outer_kernel([(dy, hidden)], after(my_side, y_parts[0]), d_got, "d_grads")
    d_total = scatter_rows(d_sums)
    gu_pairs = [(normed_mid, dgate), (normed_mid, dup)]
    gu_theirs = outer_kernel(gu_pairs, after(other_side, d_sums), None, "gu_grads_theirs")
    gu_got = core_swap(gu_theirs)
    mid_got[0] = after(mid_got[0], gu_theirs, *query_slots[1:])
    branch_rows, ffn_gain_term = norm_mid_back_kernel(
        [mid_parts[0]] + mid_got, resid, inv_mid, gain_mid, dy, spot
    )
    branch_units = head_gather(branch_rows)
    g_sums, u_sums = outer_kernel(gu_pairs, after(my_side, branch_rows), gu_got, "gu_grads", split=True)
    g_total = scatter_rows(g_sums)
    branch_units[0] = after(branch_units[0], d_total)
    branch = place_rows(
        branch_units, jnp.stack([head ^ k for k in range(n_head)]).astype(jnp.int32), n_head
    )

    grads, head_sums = head_back_kernel(
        branch, kvqo_w, 3 * cols, cols, unit_head, out_two, finish, gain_heads[:, None], lam
    )
    grad_slots = [grads]

    for slot in range(1, reach):
        grad_slots.append(lax.ppermute(grads, "ctx", downward[slot]))

    def back(slot, finish, on, sums, *gates):
        block_low, block_meta = low, meta
        if on:
            block_low, block_meta = reach_of(place + slot, starts_of(place + slot))
        return attend_back_kernel(
            slot,
            finish,
            after(block_meta, *gates),
            lam,
            query_slots[slot] if on else queries,
            kv if on else kv_slots[slot],
            block_low,
            grad_slots[slot] if on else grads,
            (cosine, sine),
            sums,
        )

    y_got = [head_move(after(y_parts[k], branch), k) for k in range(1, n_head)]
    only = reach == 1
    dq, dkv = back(0, (only, only), False, (None, None))
    last = dq
    for slot in reversed(range(1, reach)):
        arrived = [grad_slots[1]] + y_got if slot == 1 else []
        dq = back(slot, (slot == 1, False), False, (dq, False), last, *arrived)[0]
        last = dq
    dq_pre = dq

    my_cols = head * slice_width
    output = lax.dynamic_slice_in_dim(resid, my_cols, slice_width, 1) + after(y_parts[0], dq_pre).astype(F32)
    for got in y_got:
        output = output + got.astype(F32)
    output = output.astype(BF16)
    last = output
    for slot in range(1, reach):
        dkv = back(slot, (False, slot == reach - 1), True, (False, dkv), last)[0]
        last = dkv
        if slot == 1:
            u_sums = after(u_sums, dkv)
    u_total = scatter_rows(after(u_sums, g_total, *grad_slots))
    dkv_pre = dkv

    oqkv_pairs = [(branch, head_out), (normed_in, dq_pre), (normed_in, dkv_pre)]
    oqkv_theirs = outer_kernel(oqkv_pairs, other_side, None, "oqkv_grads_theirs")
    oqkv_got = core_swap(oqkv_theirs)
    in_parts = quarters_kernel(
        [(dq_pre, kvqo_w, 2 * cols), (dkv_pre, kvqo_w, 0)],
        after(spot, oqkv_theirs),
        n_head,
        "in_back",
        norm=(x_full, inv_in, gain_in),
    )
    oqkv_sums = outer_kernel(oqkv_pairs, after(my_side, in_parts[0]), oqkv_got, "oqkv_grads")
    oqkv_total = scatter_rows(after(oqkv_sums, u_total))
    oq_total, kv_total = oqkv_total[:, : 2 * cols], oqkv_total[:, 2 * cols :]
    head_sums = jnp.sum(head_sums.reshape(heads, VD, 128), axis=0)
    small = jnp.concatenate(
        [
            in_parts[n_head][0],
            ffn_gain_term[0],
            head_sums[:, 0],
            jnp.full((128,), jnp.sum(head_sums[:, 1]), F32),
        ]
    ).reshape(-1, 128)
    small = line_sum(small)
    in_got = [head_move(in_parts[k], k) for k in range(1, n_head)]
    grad_in = jnp.zeros((rows + 16, slice_width), F32)
    for got in [in_parts[0]] + in_got:
        grad_in = grad_in + got.astype(F32)
    count = rows // slice_width
    row_sums = (grad_in[rows : rows + count] + grad_in[rows + count : rows + 2 * count]).reshape(rows, 1)
    grad_in = grad_in[:rows]
    my_gain = lax.dynamic_slice_in_dim(gain_in, my_cols, slice_width, 1)
    my_branch = lax.dynamic_slice_in_dim(branch, my_cols, slice_width, 1).astype(F32)
    unit_in = tokens.astype(F32) * inv_in
    grad_tokens = my_branch + inv_in * (grad_in * my_gain - unit_in * (row_sums / wide))

    small = head_sum(after(small, *in_got)).reshape(-1)
    attn_gain_grad = small[:wide]
    ffn_gain_grad = small[wide : 2 * wide]
    heads_gain_grad = small[2 * wide : 2 * wide + VD]
    lambda_scalar = small[2 * wide + VD]
    grad_lambda = jnp.stack(
        [
            lambda_scalar * exp_one * lambda_vec[1],
            lambda_scalar * exp_one * lambda_vec[0],
            -lambda_scalar * exp_two * lambda_vec[3],
            -lambda_scalar * exp_two * lambda_vec[2],
        ],
        axis=0,
    )
    grad_kv = kv_total.astype(F32)
    grad_key = jnp.concatenate([grad_kv[:, 2 * h * VD : (2 * h + 1) * VD] for h in range(heads)], axis=1)
    grad_value = jnp.concatenate(
        [grad_kv[:, (2 * h + 1) * VD : (2 * h + 2) * VD] for h in range(heads)], axis=1
    )
    return (
        output,
        grad_tokens,
        attn_gain_grad,
        oq_total[:, cols:].astype(F32),
        grad_key,
        grad_value,
        oq_total[:, :cols].astype(F32).T,
        grad_lambda,
        heads_gain_grad,
        ffn_gain_grad,
        g_total.astype(F32),
        u_total.astype(F32),
        d_total.astype(F32).T,
    )


def solution(mesh):
    split = P(("dp", "ctx"), "head")
    turned = P("head", ("dp", "ctx"))
    in_specs = (
        split,
        P("dp"),
        P(),
        split,
        split,
        split,
        turned,
        P(),
        P(),
        P(),
        split,
        split,
        turned,
        split,
    )
    out_specs = (
        split,
        split,
        P(),
        split,
        split,
        split,
        turned,
        P(),
        P(),
        P(),
        split,
        split,
        turned,
    )
    return jax.shard_map(
        per_device, mesh=mesh, in_specs=in_specs, out_specs=out_specs, check_vma=False
    )
```
